32 devices in a mesh: lat: 4 (over y, x), lon: 8 (over z, core).
Axes of the slice: x: 2, y: 2, z: 4, core: 2. Of those that a mesh axis runs over, the one named last changes fastest.
Arguments:
- state: float32 [8, 60, 32, 1024], P(None, None, 'lat', 'lon'), may hold values from -6 to 6
- surface: bfloat16 [76, 32, 1024], P(None, 'lat', 'lon'), may hold values from -6 to 6
- layer_one: bfloat16 [556, 768], replicated, may hold values from -0.25 to 0.25
- layer_two: bfloat16 [768, 640], replicated, may hold values from -0.21875 to 0.21875
- layer_three: bfloat16 [640, 512], replicated, may hold values from -0.25 to 0.25
- layer_four: bfloat16 [512, 640], replicated, may hold values from -0.25 to 0.25
- layer_five: bfloat16 [640, 368], replicated, may hold values from -0.25 to 0.25
- lit_columns: int32 [4, 8, 1024], P('lat', 'lon'), may hold values from 0 to 1024, as said below
- row_offset: int32 [32], P('lat'), may hold values from 0 to 383
Outputs:
- new_state: float32 [8, 60, 32, 1024], P(None, None, 'lat', 'lon')
- surface_flux: bfloat16 [8, 32, 1024], P(None, 'lat', 'lon')
The draws below stay inside these ranges and needn't reach their ends.
Inputs may be any that keep to these rules, and one draw needn't show every extreme that they name: `lit_columns`: in each tile's list the first entries are distinct column numbers in rising order and the rest equal 1024. A tile and the tile 8/2 further along the longitude cycle, in the same latitude tile, list 1024 columns together at most, and some such pair lists exactly 1024 in every draw.
All inputs are finite; a program needn't handle non-finite values.
Results may differ from the reference program's by a relative error of at most 0.015.
Values may be sent and summed in bfloat16 or wider, within the bound.
No kernel may reach another device: no remote copies, remote signals or barrier semaphores. Data moves between devices by JAX's collectives and lax.ppermute only.
A program may use at most 64 MiB of HBM per device.

```python
import jax
import jax.numpy as jnp
from jax import lax

CLAT = 8
CLON = 128
LEV = 60
SUBSTEPS = 4
REACH = 2
NSURF = 76
NFLUX = 8
H1 = 768
H2 = 640
H3 = 512
H4 = 640
NIN = 556
NOUT = 368
CPT = 1024
HALF = 512
NLAT = 32
NLON = 1024
N_LAT = 4
N_LON = 8


def draw_lit_columns(key, part):
    key_total, key_share, key_full, key_sun, key_perm = jax.random.split(jax.random.fold_in(key, 11), 5)
    half_cycle = N_LON // 2
    pair_total = jax.random.randint(key_total, (N_LAT, half_cycle), CPT // 2, CPT + 1)
    full_pair = jax.random.randint(key_full, (), 0, N_LAT * half_cycle)
    pair_total = pair_total.reshape(-1).at[full_pair].set(CPT).reshape(N_LAT, half_cycle)
    night_count = jax.random.randint(key_share, (N_LAT, half_cycle), 0, pair_total // 4 + 1)
    day_count = pair_total - night_count
    sun_place = jax.random.randint(key_sun, (), 0, N_LON)
    first_half = jnp.arange(half_cycle, dtype=jnp.int32)
    first_lit = (first_half - sun_place) % N_LON < half_cycle
    first_count = jnp.where(first_lit[None, :], day_count, night_count)
    second_count = jnp.where(first_lit[None, :], night_count, day_count)
    counts = jnp.concatenate([first_count, second_count], axis=1)
    tile_keys = jax.random.split(key_perm, N_LAT * N_LON)
    shuffled = jax.vmap(lambda tile_key: jax.random.permutation(tile_key, CPT))(tile_keys).reshape(N_LAT, N_LON, CPT)
    position = jnp.arange(CPT, dtype=jnp.int32)
    chosen = jnp.where(position[None, None, :] < counts[:, :, None], shuffled, CPT)
    return jnp.sort(chosen, axis=-1).astype(jnp.int32)


def set_ends(values, key, smallest, largest):
    dims = values.shape
    spot = [jax.random.randint(jax.random.fold_in(key, axis), (), 0, dims[axis]) for axis in range(len(dims))]
    values = values.at[tuple(spot)].set(smallest)
    longest = dims.index(max(dims))
    spot[longest] = (spot[longest] + 1) % dims[longest]
    return values.at[tuple(spot)].set(largest)


def level_of(rng, shape, cuts, smallest, high):
    def one(axis_at, parts):
        heights = jax.random.uniform(jax.random.fold_in(jax.random.fold_in(rng, 6), axis_at), (parts,), jnp.float32, smallest / len(cuts), high / len(cuts))
        return jnp.repeat(jnp.exp(heights), shape[axis_at] // parts).reshape((-1,) + (1,) * (len(shape) - axis_at - 1))

    factor_of = one(*cuts[0])
    for cut in cuts[1:]:
        factor_of = factor_of * one(*cut)
    return factor_of


def bell_draw(own_key, extent, spread, limit, shards=(), held_as=jnp.bfloat16):
    gain = level_of(own_key, extent, shards, -0.22, 0.18) if shards else 1.0
    array = jax.random.normal(own_key, extent, jnp.float32) * spread * gain
    return jnp.minimum(jnp.maximum(array, -limit), limit).astype(held_as)


def setup_inputs(seed: int = 0) -> dict:
    arg_keys = jax.random.split(jax.random.key(seed), 10)
    return {
        "state": bell_draw(arg_keys[0], (8, LEV, NLAT, NLON), 1.0, 6.0, ((2, 4), (3, 8)), jnp.float32),
        "surface": bell_draw(arg_keys[1], (NSURF, NLAT, NLON), 1.0, 6.0, ((1, 4), (2, 8))),
        "layer_one": bell_draw(arg_keys[2], (NIN, H1), NIN ** -0.5, 0.25),
        "layer_two": bell_draw(arg_keys[3], (H1, H2), H1 ** -0.5, 0.21875),
        "layer_three": bell_draw(arg_keys[4], (H2, H3), H2 ** -0.5, 0.25),
        "layer_four": bell_draw(arg_keys[5], (H3, H4), H3 ** -0.5, 0.25),
        "layer_five": bell_draw(arg_keys[6], (H4, NOUT), H4 ** -0.5, 0.25),
        "lit_columns": draw_lit_columns(jax.random.fold_in(arg_keys[9], 71), 0),
        "row_offset": set_ends(jax.random.randint(arg_keys[8], (NLAT,), 0, (REACH + 1) * CLON), jax.random.fold_in(arg_keys[8], 1), 0, ((REACH + 1) * CLON) - 1).astype(jnp.int32),
    }


SOUND_COURANT = 0.6
PHYSICS_STEP = 0.5
LEAK_SLOPE = 0.15


def run_network(inputs, layers):
    hidden = inputs
    for weight in layers[:-1]:
        summed = lax.dot_general(weight, hidden, (((0,), (0,)), ((), ())), preferred_element_type=jnp.float32)
        hidden = jnp.maximum(summed, LEAK_SLOPE * summed).astype(jnp.bfloat16)
    summed = lax.dot_general(layers[-1], hidden, (((0,), (0,)), ((), ())), preferred_element_type=jnp.float32)
    return summed.astype(jnp.bfloat16)


def mark_lit(listing):
    return jnp.zeros((CPT + 1,), jnp.float32).at[listing].set(1.0)[:CPT]


def reference(state, surface, layer_one, layer_two, layer_three, layer_four, layer_five, lit_columns, row_offset):
    zonal_wind, merid_wind, pressure = state[0], state[1], state[2]
    lat_rows = jnp.arange(NLAT, dtype=jnp.int32)
    north_open = (lat_rows < NLAT - 1).astype(jnp.float32)[None, :, None]
    for substep in range(SUBSTEPS):
        zonal_wind = zonal_wind - SOUND_COURANT * (jnp.roll(pressure, -1, axis=2) - pressure)
        north_row = jnp.concatenate([pressure[:, 1:], jnp.zeros_like(pressure[:, :1])], axis=1)
        merid_wind = (merid_wind - SOUND_COURANT * (north_row - pressure)) * north_open
        south_row = jnp.concatenate([jnp.zeros_like(merid_wind[:, :1]), merid_wind[:, :-1]], axis=1)
        pressure = pressure - SOUND_COURANT * (zonal_wind - jnp.roll(zonal_wind, 1, axis=2) + merid_wind - south_row)
    all_columns = NLAT * NLON
    dynamics = jnp.stack([zonal_wind, merid_wind, pressure]).reshape(3 * LEV, all_columns)
    features = jnp.concatenate([dynamics, state[3:].reshape(5 * LEV, all_columns), surface.astype(jnp.float32).reshape(NSURF, all_columns)], axis=0).astype(jnp.bfloat16)
    lit_mask = jax.vmap(jax.vmap(mark_lit))(lit_columns)
    lit_mask = lit_mask.reshape(N_LAT, N_LON, CLAT, CLON).transpose(0, 2, 1, 3).reshape(all_columns)
    lit_index = jnp.nonzero(lit_mask > 0.5, size=all_columns // 2, fill_value=all_columns)[0].astype(jnp.int32)
    picked = jnp.take(features, jnp.minimum(lit_index, all_columns - 1), axis=1)
    batches = picked.reshape(NIN, all_columns // 2 // HALF, HALF).transpose(1, 0, 2)
    layers = (layer_one, layer_two, layer_three, layer_four, layer_five)
    physics_out = lax.map(lambda batch: run_network(batch, layers), batches)
    physics_out = physics_out.transpose(1, 0, 2).reshape(NOUT, all_columns // 2)
    results = jnp.zeros((NOUT, all_columns + 1), jnp.bfloat16).at[:, lit_index].set(physics_out)[:, :all_columns]
    tendency = results[:6 * LEV].astype(jnp.float32).reshape(6, LEV, NLAT, NLON)
    surface_flux = results[6 * LEV:].reshape(NFLUX, NLAT, NLON)
    updated_zonal = zonal_wind + PHYSICS_STEP * tendency[0]
    updated_merid = merid_wind + PHYSICS_STEP * tendency[1]
    scalars = state[3:] + PHYSICS_STEP * jnp.concatenate([tendency[2:], jnp.zeros_like(tendency[:1])], axis=0)
    fraction = 0.5 + 0.45 * jnp.tanh(zonal_wind)
    fraction_west = jnp.roll(fraction, 1, axis=2)
    source_index = (jnp.arange(NLON, dtype=jnp.int32)[None, :] - row_offset[:, None]) % NLON

    def advect(tracer):
        near_index = jnp.broadcast_to(source_index, tracer.shape)
        far_index = (near_index - 1) % NLON
        near_value = jnp.take_along_axis(tracer, near_index, axis=2)
        far_value = jnp.take_along_axis(tracer, far_index, axis=2)
        return (1.0 - fraction) * near_value + fraction_west * far_value

    advected = lax.map(advect, scalars)
    new_state = jnp.concatenate([jnp.stack([updated_zonal, updated_merid, pressure]), advected], axis=0)
    return new_state, surface_flux
```

```python
import functools

import jax
import jax.numpy as jnp
from jax import lax
from jax.experimental import pallas as pl
from jax.experimental.pallas import tpu as pltpu
from jax.sharding import PartitionSpec as P

SUBSTEPS = 4
SOUND_COURANT = 0.6
PHYSICS_STEP = 0.5
LEAK_SLOPE = 0.15

STRIP = 6 * SUBSTEPS
F32 = jnp.float32
BF16 = jnp.bfloat16


def vmem():
    return pl.BlockSpec(memory_space=pltpu.VMEM)


def any_space():
    return pl.BlockSpec(memory_space=pl.ANY)


def params(mib):
    return pltpu.CompilerParams(vmem_limit_bytes=mib << 20)


def cost(flops, nbytes):
    return pl.CostEstimate(flops=flops, bytes_accessed=nbytes, transcendentals=0)


def iota(shape, dim):
    return lax.broadcasted_iota(jnp.int32, shape, dim)


def back(shift, size):
    return (size - shift) % size


def pack_rows_kernel(state_ref, south_ref, north_ref, ozone_ref):
    levels = 3 * state_ref.shape[1]
    rows, cols = state_ref.shape[2:]
    low = iota((rows, cols), 0) < rows // 2
    flat = state_ref.reshape(state_ref.shape[0] * state_ref.shape[1], rows, cols)

    def body(step, carry):
        block = flat[pl.ds(step * 20, 20)].reshape(10, 2, rows, cols)
        even = block[:, 0]
        odd = pltpu.roll(block[:, 1], rows // 2, 1)
        south = jnp.where(low, even, odd)
        north = jnp.where(low, odd, even)
        south_ref[pl.ds(step * 5, 5)] = south.reshape(5, 2 * rows, cols).astype(BF16)
        north_ref[pl.ds(step * 5, 5)] = north.reshape(5, 2 * rows, cols).astype(BF16)
        return carry

    lax.fori_loop(0, levels // 20, body, 0)
    count = state_ref.shape[1]
    last = state_ref[state_ref.shape[0] - 1]
    ozone_ref[...] = last.reshape(count // 2, 2 * rows, cols).astype(BF16)


def pack_rows(state):
    fields, levels, rows, cols = state.shape
    half = jax.ShapeDtypeStruct((3 * levels // 4, 2 * rows, cols), BF16)
    return pl.pallas_call(
        pack_rows_kernel,
        out_shape=(half, half, jax.ShapeDtypeStruct((levels // 2, 2 * rows, cols), BF16)),
        in_specs=[vmem()],
        out_specs=(vmem(), vmem(), vmem()),
        compiler_params=params(8),
        cost_estimate=cost(1 << 20, 4 << 20),
    )(state)


def halo_rows(north_pair, south_pair, low):
    even = jnp.where(low, north_pair, south_pair)
    odd = pltpu.roll(jnp.where(low, south_pair, north_pair), north_pair.shape[-2] // 2, 1)
    return even, odd


def pack_cols_kernel(state_ref, from_north_ref, from_south_ref, west_ref, east_ref):
    levels = state_ref.shape[1]
    rows, cols = state_ref.shape[2:]
    per = cols // STRIP
    low = iota((rows, cols), 0) < rows // 2
    lane = iota((2 * rows, cols), 1)
    flat = state_ref.reshape(state_ref.shape[0] * levels, rows, cols)

    def body(step, carry):
        own = flat[pl.ds(step * 20, 20)]
        north = from_north_ref[pl.ds(step * 5, 5)].astype(F32).reshape(10, rows, cols)
        south = from_south_ref[pl.ds(step * 5, 5)].astype(F32).reshape(10, rows, cols)
        even, odd = halo_rows(north, south, low)
        west_out, east_out = [], []
        for pack in range(4):
            west = jnp.zeros((2 * rows, cols), F32)
            east = jnp.zeros((2 * rows, cols), F32)
            for slot in range(per):
                level = pack * per + slot
                side = (odd if level % 2 else even)[level // 2]
                tile = jnp.concatenate([own[level], side], axis=0)
                start = slot * STRIP
                inside = (lane >= start) & (lane < start + STRIP)
                west = jnp.where(inside, pltpu.roll(tile, start + 2 * SUBSTEPS, 1), west)
                east = jnp.where(inside, pltpu.roll(tile, start + 4 * SUBSTEPS, 1), east)
            west_out.append(west)
            east_out.append(east)
        west_ref[pl.ds(step * 4, 4)] = jnp.stack(west_out).astype(BF16)
        east_ref[pl.ds(step * 4, 4)] = jnp.stack(east_out).astype(BF16)
        return carry

    lax.fori_loop(0, 3 * levels // 20, body, 0)


def pack_cols(state, from_north, from_south):
    fields, levels, rows, cols = state.shape
    packs = 3 * levels // (cols // STRIP)
    strip = jax.ShapeDtypeStruct((packs, 2 * rows, cols), BF16)
    return pl.pallas_call(
        pack_cols_kernel,
        out_shape=(strip, strip),
        in_specs=[vmem()] * 3,
        out_specs=(vmem(), vmem()),
        compiler_params=params(8),
        cost_estimate=cost(1 << 20, 4 << 20),
    )(state, from_north, from_south)


def open_rows(rows, cols):
    place = iota((2 * rows, cols), 0)
    offset = jnp.where(place < rows + rows // 2, place, place - 2 * rows)
    row = lax.axis_index("lat") * rows + offset
    last = rows * lax.axis_size("lat") - 1
    return jnp.where((row >= 0) & (row < last), 1.0, 0.0).astype(F32)


def substeps(zonal, merid, press, free):
    rows, cols = zonal.shape[-2:]
    for _ in range(SUBSTEPS):
        zonal = zonal - SOUND_COURANT * (pltpu.roll(press, cols - 1, 2) - press)
        merid = (merid - SOUND_COURANT * (pltpu.roll(press, rows - 1, 1) - press)) * free
        press = press - SOUND_COURANT * (
            zonal - pltpu.roll(zonal, 1, 2) + merid - pltpu.roll(merid, 1, 1)
        )
    return zonal, merid, press


def inner_kernel(state_ref, from_north_ref, from_south_ref, out_ref):
    levels = state_ref.shape[1]
    rows, cols = state_ref.shape[2:]
    low = iota((rows, cols), 0) < rows // 2
    free = open_rows(rows, cols)

    def body(step, carry):
        parts = []
        for field in range(3):
            own = state_ref[field, pl.ds(step * 4, 4)]
            at = field * (levels // 4) + step
            north = from_north_ref[at].astype(F32).reshape(2, rows, cols)
            south = from_south_ref[at].astype(F32).reshape(2, rows, cols)
            even, odd = halo_rows(north, south, low)
            side = jnp.stack([even[0], odd[0], even[1], odd[1]])
            parts.append(jnp.concatenate([own, side], axis=1))
        for field, value in enumerate(substeps(*parts, free)):
            out_ref[field, pl.ds(step * 4, 4)] = value[:, :rows]
        return carry

    lax.fori_loop(0, levels // 4, body, 0)


def inner(state, from_north, from_south):
    fields, levels, rows, cols = state.shape
    return pl.pallas_call(
        inner_kernel,
        out_shape=jax.ShapeDtypeStruct((3, levels, rows, cols), F32),
        in_specs=[vmem()] * 3,
        out_specs=vmem(),
        compiler_params=params(8),
        cost_estimate=cost(1 << 24, 4 << 20),
    )(state, from_north, from_south)


def rest_kernel(state_ref, surface_ref, slots_ref, rest_ref, lit_ref, buffer, wide):
    fields, levels, rows, cols = state_ref.shape
    extra = surface_ref.shape[0]
    first = 3 * levels
    wide[...] = surface_ref[...].astype(F32).reshape(extra * rows, cols)
    flat = state_ref.reshape(fields * levels * rows, cols)
    buffer[0:first] = jnp.zeros((first, cols), F32)
    for row in range(rows):
        buffer[first : fields * levels] = flat[
            pl.ds(first * rows + row, (fields - 3) * levels, stride=rows), :
        ]
        buffer[fields * levels : fields * levels + extra] = wide[pl.ds(row, extra, stride=rows), :]
        rest_ref[:, row * cols : (row + 1) * cols] = buffer[...].astype(BF16)
    slots = slots_ref[...]
    count = slots.shape[1]
    in_row = (slots // cols == iota((rows, count), 0)).astype(F32).astype(BF16)
    in_col = (slots % cols == iota((cols, count), 0)).astype(F32).astype(BF16)
    lit_ref[...] = lax.dot_general(
        in_row, in_col, (((1,), (1,)), ((), ())), preferred_element_type=F32
    )


def rest_features(state, surface, slots):
    fields, levels, rows, cols = state.shape
    count = fields * levels + surface.shape[0]
    return pl.pallas_call(
        rest_kernel,
        out_shape=(
            jax.ShapeDtypeStruct((count, rows * cols), BF16),
            jax.ShapeDtypeStruct((rows, cols), F32),
        ),
        in_specs=[vmem()] * 3,
        out_specs=(vmem(), vmem()),
        scratch_shapes=[
            pltpu.VMEM((count, cols), F32),
            pltpu.VMEM((surface.shape[0] * rows, cols), F32),
        ],
        compiler_params=params(12),
        cost_estimate=cost(1 << 24, 4 << 20),
    )(state, surface, slots)


def leaky(value):
    return jnp.maximum(value, LEAK_SLOPE * value).astype(BF16)


def tracer_update(weight, hidden, lit, state_at, out_ref, spread):
    rows, cols = lit.shape
    levels = weight.shape[0]
    result = lax.dot_general(
        weight, hidden, (((1,), (1,)), ((), ())), preferred_element_type=F32
    )
    for row in range(rows):
        spread[pl.ds(row, levels, stride=rows), :] = result[:, row * cols : (row + 1) * cols]

    def body(step, carry):
        value = spread[pl.ds(step * 10 * rows, 10 * rows), :].reshape(10, rows, cols)
        value = jnp.where(lit > 0.5, value.astype(BF16).astype(F32), 0.0)
        value = state_at(step) + PHYSICS_STEP * value
        out_ref[pl.ds(step * 5, 5)] = value.reshape(5, 2 * rows, cols).astype(BF16)
        return carry

    lax.fori_loop(0, levels // 10, body, 0)


def network_kernel(
    inner_ref,
    own_west_ref,
    own_east_ref,
    from_east_ref,
    from_west_ref,
    rest_ref,
    one_ref,
    two_ref,
    three_ref,
    four_ref,
    five_ref,
    lit_ref,
    state_ref,
    winds_ref,
    upwind_ref,
    hidden_ref,
    tracer_ref,
    strips,
    spread,
    features,
):
    fields, levels, rows, cols = inner_ref.shape
    per = cols // STRIP
    packs = levels // per
    place = iota((2 * rows, cols), 1) % STRIP
    free = open_rows(rows, cols)

    def side(step, carry):
        parts = []
        for field in range(3):
            at = pl.ds(field * packs + step * 4, 4)
            value = jnp.where(
                place < 2 * SUBSTEPS,
                own_west_ref[at].astype(F32),
                jnp.where(
                    place < 3 * SUBSTEPS,
                    from_east_ref[at].astype(F32),
                    jnp.where(
                        place < 4 * SUBSTEPS,
                        from_west_ref[at].astype(F32),
                        own_east_ref[at].astype(F32),
                    ),
                ),
            )
            parts.append(value)
        for field, value in enumerate(substeps(*parts, free)):
            strips[field, pl.ds(step * 4, 4)] = value[:, :rows]
        return carry

    lax.fori_loop(0, packs // 4, side, 0)
    lane = iota((rows, cols), 1)

    def merge(step, carry):
        for slot in range(per):
            level = step * per + slot
            for field in range(3):
                strip = strips[field, step]
                west = pltpu.roll(strip, back(slot * STRIP + 4 * SUBSTEPS, cols), 1)
                east = pltpu.roll(strip, back(slot * STRIP + 2 * SUBSTEPS, cols), 1)
                value = inner_ref[field, level]
                value = jnp.where(lane < SUBSTEPS, west, value)
                value = jnp.where(lane >= cols - SUBSTEPS, east, value)
                winds_ref[pl.ds((field * levels + level) * rows, rows), :] = value
                if field == 0:
                    upwind_ref[level] = pltpu.roll(jnp.where(lane == cols - 1, west, value), 1, 1)
        return carry

    lax.fori_loop(0, packs, merge, 0)
    count = 3 * levels
    features[...] = rest_ref[...]
    for row in range(rows):
        features[0:count, row * cols : (row + 1) * cols] = winds_ref[
            pl.ds(row, count, stride=rows), :
        ].astype(BF16)
    total = rows * cols
    chunk = total // 2

    for part in range(2):
        at = part * chunk
        hidden = leaky(
            lax.dot_general(
                features[:, at : at + chunk],
                one_ref[...],
                (((0,), (0,)), ((), ())),
                preferred_element_type=F32,
            )
        )
        for weight in (two_ref, three_ref, four_ref):
            hidden = leaky(jnp.dot(hidden, weight[...], preferred_element_type=F32))
        hidden_ref[at : at + chunk] = hidden
    size = five_ref.shape[0]
    tracer_update(
        five_ref[...],
        hidden_ref[...],
        lit_ref[...],
        lambda step: state_ref[pl.ds(step * 10, 10)],
        tracer_ref,
        spread,
    )


def network(inner_out, strips, rest, layers, five, lit, tracers):
    fields, levels, rows, cols = inner_out.shape
    count = five.shape[0]
    width = layers[3].shape[1]
    return pl.pallas_call(
        network_kernel,
        out_shape=(
            jax.ShapeDtypeStruct((3 * levels * rows, cols), F32),
            jax.ShapeDtypeStruct((levels, rows, cols), F32),
            jax.ShapeDtypeStruct((rows * cols, width), BF16),
            jax.ShapeDtypeStruct((count // 2, 2 * rows, cols), BF16),
        ),
        in_specs=[vmem()] * 13,
        out_specs=(vmem(),) * 4,
        scratch_shapes=[
            pltpu.VMEM((3, levels * STRIP // (cols - cols % STRIP), rows, cols), F32),
            pltpu.VMEM((count * rows, cols), F32),
            pltpu.VMEM(rest.shape, BF16),
        ],
        compiler_params=params(32),
        cost_estimate=cost(4 << 30, 8 << 20),
    )(inner_out, *strips, rest, *layers, five, lit, tracers)


def second_kernel(hidden_ref, five_ref, lit_ref, state_ref, tracer_ref, spread):
    tracer_update(
        five_ref[...],
        hidden_ref[...],
        lit_ref[...],
        lambda step: state_ref[pl.ds(step * 10, 10)],
        tracer_ref,
        spread,
    )


def second(hidden, five, lit, tracers):
    rows, cols = lit.shape
    count = five.shape[0]
    return pl.pallas_call(
        second_kernel,
        out_shape=jax.ShapeDtypeStruct((count // 2, 2 * rows, cols), BF16),
        in_specs=[vmem()] * 4,
        out_specs=vmem(),
        scratch_shapes=[pltpu.VMEM((count * rows, cols), F32)],
        compiler_params=params(16),
        cost_estimate=cost(1 << 28, 3 << 20),
    )(hidden, five, lit, tracers)


def winds_kernel(
    hidden_ref, five_ref, lit_ref, winds_ref, upwind_ref, out_ref, flux_ref, stay_ref, come_ref,
    spread, updated, sem
):
    rows, cols = lit_ref.shape
    levels = upwind_ref.shape[0]
    fluxes = flux_ref.shape[0]
    result = lax.dot_general(
        five_ref[...], hidden_ref[...], (((1,), (1,)), ((), ())), preferred_element_type=F32
    )
    count = five_ref.shape[0]
    for row in range(rows):
        spread[pl.ds(row, count, stride=rows), :] = result[:, row * cols : (row + 1) * cols]
    lit = lit_ref[...] > 0.5

    def body(step, carry):
        value = spread[pl.ds(step * 10 * rows, 10 * rows), :].reshape(10, rows, cols)
        value = jnp.where(lit, value.astype(BF16).astype(F32), 0.0)
        wind = winds_ref[pl.ds(step * 10 * rows, 10 * rows), :].reshape(10, rows, cols)
        updated[pl.ds(step * 10, 10)] = wind + PHYSICS_STEP * value
        return carry

    lax.fori_loop(0, 2 * levels // 10, body, 0)
    updated[2 * levels : 3 * levels] = winds_ref[2 * levels * rows :, :].reshape(
        levels, rows, cols
    )
    copy = pltpu.make_async_copy(
        updated, out_ref.at[pl.ds(0, 3 * levels)], sem
    )
    copy.start()
    value = spread[2 * levels * rows :, :].reshape(fluxes, rows, cols)
    flux_ref[...] = jnp.where(lit, value, 0.0).astype(BF16)

    def share(step, carry):
        here = winds_ref[pl.ds(step * 10 * rows, 10 * rows), :].reshape(10, rows, cols)
        stay_ref[pl.ds(step * 10, 10)] = 0.5 - 0.45 * jnp.tanh(here)
        come_ref[pl.ds(step * 10, 10)] = 0.5 + 0.45 * jnp.tanh(upwind_ref[pl.ds(step * 10, 10)])
        return carry

    lax.fori_loop(0, levels // 10, share, 0)
    copy.wait()


def winds_out(hidden, five, lit, winds, upwind, fields):
    levels, rows, cols = upwind.shape
    fluxes = five.shape[0] - 2 * levels
    share = jax.ShapeDtypeStruct((levels, rows, cols), F32)
    return pl.pallas_call(
        winds_kernel,
        out_shape=(
            jax.ShapeDtypeStruct((fields * levels, rows, cols), F32),
            jax.ShapeDtypeStruct((fluxes, rows, cols), BF16),
            share,
            share,
        ),
        in_specs=[vmem()] * 5,
        out_specs=(any_space(), vmem(), vmem(), vmem()),
        scratch_shapes=[
            pltpu.VMEM((five.shape[0] * rows, cols), F32),
            pltpu.VMEM((3 * levels, rows, cols), F32),
            pltpu.SemaphoreType.DMA,
        ],
        compiler_params=params(16),
        cost_estimate=cost(1 << 28, 4 << 20),
    )(hidden, five, lit, winds, upwind)


def spread_offsets(offset_ref, rows, cols):
    place = iota((rows, cols), 0)
    offset = jnp.zeros((rows, cols), jnp.int32)
    for row in range(rows):
        offset = jnp.where(place == row, offset_ref[row], offset)
    return offset // cols, offset % cols


def along(value, index):
    return jnp.take_along_axis(value, index, axis=1, mode="promise_in_bounds")


def relay_kernel(offset_ref, own_ref, near_ref, out_ref):
    rows = own_ref.shape[1] // 2
    cols = own_ref.shape[2]
    pairs = own_ref.shape[0]
    blocks, cells = spread_offsets(offset_ref, rows, cols)
    lane = iota((rows, cols), 1)
    take_near = (blocks >= 2) & (lane > cols - 1 - cells)
    edge = cols - 1 - cells

    def body(step, column):
        at = pl.ds(step * 5, 5)
        own = own_ref[at].astype(F32).reshape(10, rows, cols)
        near = near_ref[at].astype(F32).reshape(10, rows, cols)
        out = jnp.where(take_near, near, own)
        out_ref[at] = out.reshape(5, 2 * rows, cols).astype(BF16)
        for level in range(10):
            column = jnp.where(lane == step * 10 + level, along(near[level], edge), column)
        return column

    column = lax.fori_loop(0, pairs // 5, body, jnp.zeros((rows, cols), F32))
    out_ref[pairs] = jnp.concatenate([column, column], axis=0).astype(BF16)


def relay(offset, own, near):
    pairs, height, cols = own.shape
    return pl.pallas_call(
        relay_kernel,
        out_shape=jax.ShapeDtypeStruct((pairs + 1, height, cols), BF16),
        in_specs=[pl.BlockSpec(memory_space=pltpu.SMEM), vmem(), vmem()],
        out_specs=vmem(),
        compiler_params=params(8),
        cost_estimate=cost(1 << 20, 1 << 20),
    )(offset, own, near)


def advect_kernel(
    first, offset_ref, own_ref, near_ref, far_ref, stay_ref, come_ref, whole_ref, out_ref, result, sem
):
    levels, rows, cols = stay_ref.shape
    pairs = own_ref.shape[0]
    blocks, cells = spread_offsets(offset_ref, rows, cols)
    lane = iota((rows, cols), 1)
    from_right = lane <= cols - 1 - cells
    index = (lane - cells) & (cols - 1)
    index_less = (lane - cells - 1) & (cols - 1)
    column = far_ref[pairs].astype(F32)[:rows]
    is_zero, is_one, is_two = blocks == 0, blocks == 1, blocks >= 2
    steps = levels // 10
    copies = []
    for field in range(2 * pairs // levels):
        def body(step, carry):
            at = pl.ds(field * (levels // 2) + step * 5, 5)
            own = own_ref[at].astype(F32).reshape(10, rows, cols)
            near = near_ref[at].astype(F32).reshape(10, rows, cols)
            far = far_ref[at].astype(F32).reshape(10, rows, cols)
            stay = stay_ref[pl.ds(step * 10, 10)]
            come = come_ref[pl.ds(step * 10, 10)]
            right = jnp.where(is_zero, own, jnp.where(is_one, near, far))
            left = jnp.where(is_zero, near, far)
            merged = jnp.where(from_right, right, left)
            for level in range(10):
                which = field * levels + step * 10 + level
                lone = along(column, jnp.zeros((rows, cols), jnp.int32) + which)
                edge = jnp.where(is_two, lone, left[level])
                shifted = jnp.where(lane == cols - 1 - cells, edge, merged[level])
                here = along(merged[level], index)
                behind = along(shifted, index_less)
                result[field * levels + step * 10 + level] = (
                    stay[level] * here + come[level] * behind
                )
            return carry

        lax.fori_loop(0, steps, body, 0)
        copy = pltpu.make_async_copy(
            result.at[pl.ds(field * levels, levels)],
            out_ref.at[pl.ds((first + field) * levels, levels)],
            sem.at[field],
        )
        copy.start()
        copies.append(copy)
    for copy in copies:
        copy.wait()


def advect(first, offset, own, near, far, stay, come, whole):
    pairs, height, cols = own.shape
    levels = stay.shape[0]
    return pl.pallas_call(
        functools.partial(advect_kernel, first),
        out_shape=jax.ShapeDtypeStruct(whole.shape, F32),
        in_specs=[pl.BlockSpec(memory_space=pltpu.SMEM)] + [vmem()] * 5 + [any_space()],
        out_specs=any_space(),
        scratch_shapes=[
            pltpu.VMEM((2 * pairs, height // 2, cols), F32),
            pltpu.SemaphoreType.DMA((2 * pairs // levels,)),
        ],
        input_output_aliases={6: 0},
        compiler_params=params(12),
        cost_estimate=cost(1 << 22, 3 << 20),
    )(offset, own, near, far, stay, come, whole)


def shifted(value, axis, steps):
    count = lax.axis_size(axis)
    return lax.ppermute(value, axis, [(i, (i + steps) % count) for i in range(count)])


def passed_along(block, axis, distance):
    devices = range(lax.axis_size(axis))
    return lax.ppermute(
        block, axis, [(i, i + distance) for i in devices if i + distance in devices]
    )


def on_device(
    state,
    surface,
    layer_one,
    layer_two,
    layer_three,
    layer_four,
    layer_five,
    lit_columns,
    row_offset,
):
    fields, levels, rows, cols = state.shape
    slots = lit_columns.reshape(1, rows * cols)
    flat = state.reshape(fields * levels, rows, cols)

    to_south, to_north, ozone = pack_rows(state)
    from_north = passed_along(to_south, "lat", -1)
    from_south = passed_along(to_north, "lat", 1)
    ozone_near = shifted(ozone, "lon", 1)

    rest, lit = rest_features(state, surface, slots)
    five = layer_five.T
    five_first = five[2 * levels : 4 * levels]
    five_second = five[4 * levels : 6 * levels]
    five_winds = jnp.concatenate([five[: 2 * levels], five[6 * levels :]], axis=0)

    to_west, to_east = pack_cols(state, from_north, from_south)
    from_east = shifted(to_west, "lon", -1)
    from_west = shifted(to_east, "lon", 1)
    inner_out = inner(state, from_north, from_south)
    ozone_far = shifted(relay(row_offset, ozone, ozone_near), "lon", 2)

    winds, upwind, hidden, first = network(
        inner_out,
        (to_west, to_east, from_east, from_west),
        rest,
        (layer_one, layer_two, layer_three, layer_four),
        five_first,
        lit,
        flat[3 * levels : 5 * levels],
    )
    first_near = shifted(first, "lon", 1)
    other = second(hidden, five_second, lit, flat[5 * levels : 7 * levels])
    other_near = shifted(other, "lon", 1)
    first_far = shifted(relay(row_offset, first, first_near), "lon", 2)
    other_far = shifted(relay(row_offset, other, other_near), "lon", 2)
    whole, flux, stay, come = winds_out(hidden, five_winds, lit, winds, upwind, fields)
    whole = advect(7, row_offset, ozone, ozone_near, ozone_far, stay, come, whole)
    whole = advect(3, row_offset, first, first_near, first_far, stay, come, whole)
    whole = advect(5, row_offset, other, other_near, other_far, stay, come, whole)
    return whole.reshape(fields, levels, rows, cols), flux


def solution(mesh):
    in_specs = (
        P(None, None, "lat", "lon"),
        P(None, "lat", "lon"),
        P(),
        P(),
        P(),
        P(),
        P(),
        P("lat", "lon", None),
        P("lat"),
    )
    out_specs = (P(None, None, "lat", "lon"), P(None, "lat", "lon"))
    return jax.shard_map(
        on_device, mesh=mesh, in_specs=in_specs, out_specs=out_specs, check_vma=False
    )
```

```python
import functools

import jax
import jax.numpy as jnp
from jax import lax
from jax.experimental import pallas as pl
from jax.experimental.pallas import tpu as pltpu
from jax.sharding import PartitionSpec as P


SUBSTEPS = 4
SOUND_COURANT = 0.6
PHYSICS_STEP = 0.5
LEAK_SLOPE = 0.15

STRIP = 6 * SUBSTEPS
F32 = jnp.float32
BF16 = jnp.bfloat16


def vmem():
    return pl.BlockSpec(memory_space=pltpu.VMEM)


def any_space():
    return pl.BlockSpec(memory_space=pl.ANY)


def params(mib):
    return pltpu.CompilerParams(vmem_limit_bytes=mib << 20)


def cost(flops, nbytes):
    return pl.CostEstimate(flops=flops, bytes_accessed=nbytes, transcendentals=0)


def iota(shape, dim):
    return lax.broadcasted_iota(jnp.int32, shape, dim)


def back(shift, size):
    return (size - shift) % size


def paired(tiles, rows, low):
    tiles = tiles.reshape((tiles.shape[0] // 2, 2) + tiles.shape[1:])
    even = tiles[:, 0]
    odd = pltpu.roll(tiles[:, 1], rows // 2, 1)
    return jnp.where(low, even, odd), jnp.where(low, odd, even)


def halo_rows(north_pair, south_pair, low):
    even = jnp.where(low, north_pair, south_pair)
    odd = pltpu.roll(jnp.where(low, south_pair, north_pair), north_pair.shape[-2] // 2, 1)
    return jnp.stack([even, odd], axis=1).reshape((-1,) + even.shape[1:])


def side_packs(tiles, lane):
    per = tiles.shape[-1] // STRIP
    west_packs, east_packs = [], []
    for pack in range(tiles.shape[0] // per):
        west = jnp.zeros(tiles.shape[1:], F32)
        east = jnp.zeros(tiles.shape[1:], F32)
        for slot in range(per):
            tile = tiles[pack * per + slot]
            start = slot * STRIP
            inside = (lane >= start) & (lane < start + STRIP)
            west = jnp.where(inside, pltpu.roll(tile, start + 2 * SUBSTEPS, 1), west)
            east = jnp.where(inside, pltpu.roll(tile, start + 4 * SUBSTEPS, 1), east)
        west_packs.append(west)
        east_packs.append(east)
    return jnp.stack(west_packs), jnp.stack(east_packs)


def tall(tiles):
    count, rows, cols = tiles.shape
    return tiles.reshape(count // 2, 2 * rows, cols).astype(BF16)


def messages_kernel(
    state_ref, south_ref, north_ref, west_ref, east_ref, ozone_ref, held, sems
):
    fields, levels, rows, cols = state_ref.shape
    low = iota((rows, cols), 0) < rows // 2
    lane = iota((rows, cols), 1)
    copies = []
    for place, field in enumerate((0, 1, 2, fields - 1)):
        copy = pltpu.make_async_copy(
            state_ref.at[field], held.at[pl.ds(place * levels, levels)], sems.at[place]
        )
        copy.start()
        copies.append(copy)

    def body(step, carry):
        tiles = held[pl.ds(step * 20, 20)]
        south, north = paired(tiles, rows, low)
        south_ref[pl.ds(step * 5, 5)] = tall(south)
        north_ref[pl.ds(step * 5, 5)] = tall(north)
        west, east = side_packs(tiles, lane)
        west_ref[pl.ds(step * 2, 2)] = tall(west)
        east_ref[pl.ds(step * 2, 2)] = tall(east)
        return carry

    for place in range(3):
        copies[place].wait()
        lax.fori_loop(
            place * levels // 20, (place + 1) * levels // 20, body, 0, unroll=levels // 20
        )
    copies[3].wait()
    ozone_ref[...] = tall(held[3 * levels :])


def messages(state):
    _, levels, rows, cols = state.shape

    def shape(count):
        return jax.ShapeDtypeStruct((count // 2, 2 * rows, cols), BF16)

    packs = 3 * levels // (cols // STRIP)
    return pl.pallas_call(
        messages_kernel,
        out_shape=(shape(3 * levels // 2),) * 2
        + (shape(packs),) * 2
        + (shape(levels),),
        in_specs=[pl.BlockSpec(memory_space=pltpu.HBM)],
        out_specs=(vmem(),) * 5,
        scratch_shapes=[
            pltpu.VMEM((4 * levels, rows, cols), F32),
            pltpu.SemaphoreType.DMA((4,)),
        ],
        compiler_params=pltpu.CompilerParams(vmem_limit_bytes=125 << 19),
        cost_estimate=cost(1 << 20, 4 << 20),
    )(state)


def short(ref, at, size):
    rows, cols = ref.shape[1] // 2, ref.shape[2]
    return ref[pl.ds(at // 2, size // 2)].astype(F32).reshape(size, rows, cols)


def strips_kernel(own_west_ref, own_east_ref, from_east_ref, from_west_ref, out_ref, south_ref, north_ref):
    count = 2 * own_west_ref.shape[0]
    rows, cols = own_west_ref.shape[1] // 2, own_west_ref.shape[2]
    place = iota((rows, cols), 1) % STRIP
    low = iota((rows, cols), 0) < rows // 2
    value = short(own_east_ref, 0, count)
    value = jnp.where(place < 4 * SUBSTEPS, short(from_west_ref, 0, count), value)
    value = jnp.where(place < 3 * SUBSTEPS, short(from_east_ref, 0, count), value)
    value = jnp.where(place < 2 * SUBSTEPS, short(own_west_ref, 0, count), value)
    out_ref[...] = value
    south, north = paired(value, rows, low)
    south_ref[...] = tall(south)
    north_ref[...] = tall(north)


def strips_of(own_west, own_east, from_east, from_west):
    count, height, cols = own_west.shape
    half = jax.ShapeDtypeStruct((count // 2, height, cols), BF16)
    return pl.pallas_call(
        strips_kernel,
        out_shape=(jax.ShapeDtypeStruct((2 * count, height // 2, cols), F32), half, half),
        in_specs=[vmem()] * 4,
        out_specs=(vmem(),) * 3,
        compiler_params=params(4),
        cost_estimate=cost(1 << 20, 1 << 20),
    )(own_west, own_east, from_east, from_west)


def open_rows(rows, cols):
    place = iota((2 * rows, cols), 0)
    offset = jnp.where(place < rows + rows // 2, place, place - 2 * rows)
    row = lax.axis_index("lat") * rows + offset
    last = rows * lax.axis_size("lat") - 1
    return jnp.where((row >= 0) & (row < last), 1.0, 0.0).astype(F32)


def substeps(zonal, merid, press, free):
    rows, cols = zonal.shape[-2:]
    for _ in range(SUBSTEPS):
        zonal = zonal - SOUND_COURANT * (pltpu.roll(press, cols - 1, 2) - press)
        merid = (merid - SOUND_COURANT * (pltpu.roll(press, rows - 1, 1) - press)) * free
        press = press - SOUND_COURANT * (
            zonal - pltpu.roll(zonal, 1, 2) + merid - pltpu.roll(merid, 1, 1)
        )
    return zonal, merid, press


def inner_kernel(state_ref, from_north_ref, from_south_ref, out_ref):
    levels = state_ref.shape[1]
    rows, cols = state_ref.shape[2:]
    low = iota((rows, cols), 0) < rows // 2
    free = open_rows(rows, cols)
    parts = []
    for field in range(3):
        at = pl.ds(field * (levels // 4), levels // 4)
        north = from_north_ref[at].astype(F32).reshape(levels // 2, rows, cols)
        south = from_south_ref[at].astype(F32).reshape(levels // 2, rows, cols)
        side = halo_rows(north, south, low)
        parts.append(jnp.concatenate([state_ref[field], side], axis=1))
    for field, value in enumerate(substeps(*parts, free)):
        out_ref[field] = value[:, :rows]


def inner(state, from_north, from_south):
    _, levels, rows, cols = state.shape
    return pl.pallas_call(
        inner_kernel,
        out_shape=jax.ShapeDtypeStruct((3, levels, rows, cols), F32),
        in_specs=[vmem()] * 3,
        out_specs=vmem(),
        compiler_params=params(16),
        cost_estimate=cost(1 << 24, 4 << 20),
    )(state, from_north, from_south)


def rest_kernel(state_ref, surface_ref, slots_ref, rest_ref, lit_ref, buffer, wide):
    fields, levels, rows, cols = state_ref.shape
    extra = surface_ref.shape[0]
    first = 3 * levels
    wide[...] = surface_ref[...].astype(F32).reshape(extra * rows, cols)
    flat = state_ref.reshape(fields * levels * rows, cols)
    buffer[0:first] = jnp.zeros((first, cols), F32)
    for row in range(rows):
        buffer[first : fields * levels] = flat[
            pl.ds(first * rows + row, (fields - 3) * levels, stride=rows), :
        ]
        buffer[fields * levels : fields * levels + extra] = wide[pl.ds(row, extra, stride=rows), :]
        rest_ref[:, row * cols : (row + 1) * cols] = buffer[...].astype(BF16)
    slots = slots_ref[...]
    count = slots.shape[1]
    in_row = (slots // cols == iota((rows, count), 0)).astype(F32).astype(BF16)
    in_col = (slots % cols == iota((cols, count), 0)).astype(F32).astype(BF16)
    lit_ref[...] = lax.dot_general(
        in_row, in_col, (((1,), (1,)), ((), ())), preferred_element_type=F32
    )


def rest_features(state, surface, slots):
    fields, levels, rows, cols = state.shape
    count = fields * levels + surface.shape[0]
    return pl.pallas_call(
        rest_kernel,
        out_shape=(
            jax.ShapeDtypeStruct((count, rows * cols), BF16),
            jax.ShapeDtypeStruct((rows, cols), F32),
        ),
        in_specs=[vmem()] * 3,
        out_specs=(vmem(), vmem()),
        scratch_shapes=[
            pltpu.VMEM((count, cols), F32),
            pltpu.VMEM((surface.shape[0] * rows, cols), F32),
        ],
        compiler_params=params(12),
        cost_estimate=cost(1 << 24, 4 << 20),
    )(state, surface, slots)


def leaky(value):
    return jnp.maximum(value, LEAK_SLOPE * value).astype(BF16)


def tracer_update(weight, hidden, lit, state_at, out_ref, spread):
    rows, cols = lit.shape
    levels = weight.shape[0]
    result = lax.dot_general(
        weight, hidden, (((1,), (1,)), ((), ())), preferred_element_type=F32
    )
    for row in range(rows):
        spread[pl.ds(row, levels, stride=rows), :] = result[:, row * cols : (row + 1) * cols]

    def body(step, carry):
        value = spread[pl.ds(step * 10 * rows, 10 * rows), :].reshape(10, rows, cols)
        value = jnp.where(lit > 0.5, value.astype(BF16).astype(F32), 0.0)
        value = state_at(step) + PHYSICS_STEP * value
        out_ref[pl.ds(step * 5, 5)] = value.reshape(5, 2 * rows, cols).astype(BF16)
        return carry

    lax.fori_loop(0, levels // 10, body, 0)


def network_kernel(
    parts_count,
    inner_ref,
    here_ref,
    north_ref,
    south_ref,
    rest_ref,
    one_ref,
    two_ref,
    three_ref,
    four_ref,
    five_ref,
    lit_ref,
    state_ref,
    winds_ref,
    upwind_ref,
    hidden_ref,
    tracer_ref,
    strips,
    spread,
    features,
):
    _, levels, rows, cols = inner_ref.shape
    per = cols // STRIP
    packs = levels // per
    low = iota((rows, cols), 0) < rows // 2
    free = open_rows(rows, cols)
    parts = []
    for field in range(3):
        half = [short(ref, field * packs // 2, packs // 2) for ref in (north_ref, south_ref)]
        here = here_ref[pl.ds(field * packs, packs)]
        parts.append(jnp.concatenate([here, halo_rows(*half, low)], axis=1))
    for field, value in enumerate(substeps(*parts, free)):
        strips[field] = value[:, :rows]
    lane = iota((rows, cols), 1)

    def merge(step, carry):
        for slot in range(per):
            level = step * per + slot
            for field in range(3):
                strip = strips[field, step]
                west = pltpu.roll(strip, back(slot * STRIP + 4 * SUBSTEPS, cols), 1)
                east = pltpu.roll(strip, back(slot * STRIP + 2 * SUBSTEPS, cols), 1)
                value = inner_ref[field, level]
                value = jnp.where(lane < SUBSTEPS, west, value)
                value = jnp.where(lane >= cols - SUBSTEPS, east, value)
                winds_ref[pl.ds((field * levels + level) * rows, rows), :] = value
                if field == 0:
                    upwind_ref[level] = pltpu.roll(jnp.where(lane == cols - 1, west, value), 1, 1)
        return carry

    lax.fori_loop(0, packs, merge, 0, unroll=4)
    count = 3 * levels
    features[...] = rest_ref[...]
    for row in range(rows):
        features[0:count, row * cols : (row + 1) * cols] = winds_ref[
            pl.ds(row, count, stride=rows), :
        ].astype(BF16)
    total = rows * cols
    chunk = total // parts_count

    for part in range(parts_count):
        at = part * chunk
        hidden = leaky(
            lax.dot_general(
                features[:, at : at + chunk],
                one_ref[...],
                (((0,), (0,)), ((), ())),
                preferred_element_type=F32,
            )
        )
        for weight in (two_ref, three_ref, four_ref):
            hidden = leaky(jnp.dot(hidden, weight[...], preferred_element_type=F32))
        hidden_ref[at : at + chunk] = hidden
    tracer_update(
        five_ref[...],
        hidden_ref[...],
        lit_ref[...],
        lambda step: state_ref[pl.ds(3 * levels + step * 10, 10)],
        tracer_ref,
        spread,
    )


def network(inner_out, strips, rest, layers, five, lit, tracers, parts_count=2):
    _, levels, rows, cols = inner_out.shape
    count = five.shape[0]
    width = layers[3].shape[1]
    return pl.pallas_call(
        functools.partial(network_kernel, parts_count),
        out_shape=(
            jax.ShapeDtypeStruct((3 * levels * rows, cols), F32),
            jax.ShapeDtypeStruct((levels, rows, cols), F32),
            jax.ShapeDtypeStruct((rows * cols, width), BF16),
            jax.ShapeDtypeStruct((count // 2, 2 * rows, cols), BF16),
        ),
        in_specs=[vmem()] * 12,
        out_specs=(vmem(),) * 4,
        scratch_shapes=[
            pltpu.VMEM((3, levels * STRIP // (cols - cols % STRIP), rows, cols), F32),
            pltpu.VMEM((count * rows, cols), F32),
            pltpu.VMEM(rest.shape, BF16),
        ],
        compiler_params=params(32),
        cost_estimate=cost(4 << 30, 8 << 20),
    )(inner_out, *strips, rest, *layers, five, lit, tracers)


def second_kernel(start, hidden_ref, five_ref, lit_ref, state_ref, tracer_ref, spread):
    tracer_update(
        five_ref[...],
        hidden_ref[...],
        lit_ref[...],
        lambda step: state_ref[pl.ds(start + step * 10, 10)],
        tracer_ref,
        spread,
    )


def second(start, hidden, five, lit, tracers):
    rows, cols = lit.shape
    count = five.shape[0]
    return pl.pallas_call(
        functools.partial(second_kernel, start),
        out_shape=jax.ShapeDtypeStruct((count // 2, 2 * rows, cols), BF16),
        in_specs=[vmem()] * 4,
        out_specs=vmem(),
        scratch_shapes=[pltpu.VMEM((count * rows, cols), F32)],
        compiler_params=params(16),
        cost_estimate=cost(1 << 28, 3 << 20),
    )(hidden, five, lit, tracers)


def winds_kernel(
    hidden_ref, five_ref, lit_ref, winds_ref, upwind_ref, out_ref, flux_ref, stay_ref, come_ref,
    spread, updated, sem
):
    rows, cols = lit_ref.shape
    levels = upwind_ref.shape[0]
    fluxes = flux_ref.shape[0]
    result = lax.dot_general(
        five_ref[...], hidden_ref[...], (((1,), (1,)), ((), ())), preferred_element_type=F32
    )
    count = five_ref.shape[0]
    for row in range(rows):
        spread[pl.ds(row, count, stride=rows), :] = result[:, row * cols : (row + 1) * cols]
    lit = lit_ref[...] > 0.5

    def body(step, carry):
        value = spread[pl.ds(step * 10 * rows, 10 * rows), :].reshape(10, rows, cols)
        value = jnp.where(lit, value.astype(BF16).astype(F32), 0.0)
        wind = winds_ref[pl.ds(step * 10 * rows, 10 * rows), :].reshape(10, rows, cols)
        updated[pl.ds(step * 10, 10)] = wind + PHYSICS_STEP * value
        return carry

    lax.fori_loop(0, 2 * levels // 10, body, 0)
    updated[2 * levels : 3 * levels] = winds_ref[2 * levels * rows :, :].reshape(
        levels, rows, cols
    )
    copy = pltpu.make_async_copy(
        updated, out_ref.at[pl.ds(0, 3 * levels)], sem
    )
    copy.start()
    value = spread[2 * levels * rows :, :].reshape(fluxes, rows, cols)
    flux_ref[...] = jnp.where(lit, value, 0.0).astype(BF16)

    def share(step, carry):
        here = winds_ref[pl.ds(step * 10 * rows, 10 * rows), :].reshape(10, rows, cols)
        stay_ref[pl.ds(step * 10, 10)] = 0.5 - 0.45 * jnp.tanh(here)
        come_ref[pl.ds(step * 10, 10)] = 0.5 + 0.45 * jnp.tanh(upwind_ref[pl.ds(step * 10, 10)])
        return carry

    lax.fori_loop(0, levels // 10, share, 0)
    copy.wait()


def winds_out(hidden, five, lit, winds, upwind, fields):
    levels, rows, cols = upwind.shape
    fluxes = five.shape[0] - 2 * levels
    share = jax.ShapeDtypeStruct((levels, rows, cols), F32)
    return pl.pallas_call(
        winds_kernel,
        out_shape=(
            jax.ShapeDtypeStruct((fields * levels, rows, cols), F32),
            jax.ShapeDtypeStruct((fluxes, rows, cols), BF16),
            share,
            share,
        ),
        in_specs=[vmem()] * 5,
        out_specs=(any_space(), vmem(), vmem(), vmem()),
        scratch_shapes=[
            pltpu.VMEM((five.shape[0] * rows, cols), F32),
            pltpu.VMEM((3 * levels, rows, cols), F32),
            pltpu.SemaphoreType.DMA,
        ],
        compiler_params=params(16),
        cost_estimate=cost(1 << 28, 4 << 20),
    )(hidden, five, lit, winds, upwind)


def spread_offsets(offset_ref, rows, cols):
    place = iota((rows, cols), 0)
    offset = jnp.zeros((rows, cols), jnp.int32)
    for row in range(rows):
        offset = jnp.where(place == row, offset_ref[row], offset)
    return offset // cols, offset % cols


def along(value, index):
    return jnp.take_along_axis(value, index, axis=1, mode="promise_in_bounds")


def relay_kernel(offset_ref, own_ref, near_ref, out_ref):
    rows = own_ref.shape[1] // 2
    cols = own_ref.shape[2]
    pairs = own_ref.shape[0]
    blocks, cells = spread_offsets(offset_ref, rows, cols)
    lane = iota((rows, cols), 1)
    take_near = (blocks >= 2) & (lane > cols - 1 - cells)
    edge = cols - 1 - cells

    def body(step, column):
        at = pl.ds(step * 5, 5)
        own = own_ref[at].astype(F32).reshape(10, rows, cols)
        near = near_ref[at].astype(F32).reshape(10, rows, cols)
        out = jnp.where(take_near, near, own)
        out_ref[at] = out.reshape(5, 2 * rows, cols).astype(BF16)
        for level in range(10):
            column = jnp.where(lane == step * 10 + level, along(near[level], edge), column)
        return column

    column = lax.fori_loop(0, pairs // 5, body, jnp.zeros((rows, cols), F32))
    out_ref[pairs] = jnp.concatenate([column, column], axis=0).astype(BF16)


def relay(offset, own, near):
    pairs, height, cols = own.shape
    return pl.pallas_call(
        relay_kernel,
        out_shape=jax.ShapeDtypeStruct((pairs + 1, height, cols), BF16),
        in_specs=[pl.BlockSpec(memory_space=pltpu.SMEM), vmem(), vmem()],
        out_specs=vmem(),
        compiler_params=params(8),
        cost_estimate=cost(1 << 20, 1 << 20),
    )(offset, own, near)


def advect_kernel(
    first, group, offset_ref, own_ref, near_ref, far_ref, stay_ref, come_ref, whole_ref, out_ref, result, sem
):
    levels, rows, cols = stay_ref.shape
    pairs = own_ref.shape[0]
    blocks, cells = spread_offsets(offset_ref, rows, cols)
    lane = iota((rows, cols), 1)
    from_right = lane <= cols - 1 - cells
    index = (lane - cells) & (cols - 1)
    index_less = (lane - cells - 1) & (cols - 1)
    column = far_ref[pairs].astype(F32)[:rows]
    is_zero, is_one, is_two = blocks == 0, blocks == 1, blocks >= 2
    steps = levels // group
    copies = []
    for field in range(2 * pairs // levels):
        def body(step, carry):
            at = pl.ds(field * (levels // 2) + step * (group // 2), group // 2)
            own = own_ref[at].astype(F32).reshape(group, rows, cols)
            near = near_ref[at].astype(F32).reshape(group, rows, cols)
            far = far_ref[at].astype(F32).reshape(group, rows, cols)
            stay = stay_ref[pl.ds(step * group, group)]
            come = come_ref[pl.ds(step * group, group)]
            right = jnp.where(is_zero, own, jnp.where(is_one, near, far))
            left = jnp.where(is_zero, near, far)
            merged = jnp.where(from_right, right, left)
            for level in range(group):
                which = field * levels + step * group + level
                lone = along(column, jnp.zeros((rows, cols), jnp.int32) + which)
                edge = jnp.where(is_two, lone, left[level])
                shifted = jnp.where(lane == cols - 1 - cells, edge, merged[level])
                here = along(merged[level], index)
                behind = along(shifted, index_less)
                result[field * levels + step * group + level] = (
                    stay[level] * here + come[level] * behind
                )
            return carry

        lax.fori_loop(0, steps, body, 0)
        copy = pltpu.make_async_copy(
            result.at[pl.ds(field * levels, levels)],
            out_ref.at[pl.ds((first + field) * levels, levels)],
            sem.at[field],
        )
        copy.start()
        copies.append(copy)
    for copy in copies:
        copy.wait()


def advect(first, offset, own, near, far, stay, come, whole, group=20):
    pairs, height, cols = own.shape
    levels = stay.shape[0]
    return pl.pallas_call(
        functools.partial(advect_kernel, first, group),
        out_shape=jax.ShapeDtypeStruct(whole.shape, F32),
        in_specs=[pl.BlockSpec(memory_space=pltpu.SMEM)] + [vmem()] * 5 + [any_space()],
        out_specs=any_space(),
        scratch_shapes=[
            pltpu.VMEM((2 * pairs, height // 2, cols), F32),
            pltpu.SemaphoreType.DMA((2 * pairs // levels,)),
        ],
        input_output_aliases={6: 0},
        compiler_params=params(12),
        cost_estimate=cost(1 << 22, 3 << 20),
    )(offset, own, near, far, stay, come, whole)


def shifted(value, axis, steps):
    count = lax.axis_size(axis)
    return lax.ppermute(value, axis, [(i, (i + steps) % count) for i in range(count)])


def passed_along(block, axis, distance):
    devices = range(lax.axis_size(axis))
    return lax.ppermute(
        block, axis, [(i, i + distance) for i in devices if i + distance in devices]
    )


def on_device(
    state,
    surface,
    layer_one,
    layer_two,
    layer_three,
    layer_four,
    layer_five,
    lit_columns,
    row_offset,
):
    return tile_step(
        state,
        surface,
        (layer_one, layer_two, layer_three, layer_four),
        layer_five,
        lit_columns,
        row_offset,
    )


def tile_step(state, surface, layers, layer_five, lit_columns, row_offset):
    fields, levels, rows, cols = state.shape
    slots = lit_columns.reshape(1, rows * cols)
    flat = state.reshape(fields * levels, rows, cols)

    to_south, to_north, to_west, to_east, ozone = messages(state)
    from_east = shifted(to_west, "lon", -1)
    from_west = shifted(to_east, "lon", 1)
    from_south = shifted(to_north, "lat", 1)
    from_north = passed_along(to_south, "lat", -1)
    ozone_near = shifted(ozone, "lon", 1)
    strips, strips_south, strips_north = strips_of(to_west, to_east, from_east, from_west)
    strips_from_south = shifted(strips_north, "lat", 1)
    strips_from_north = passed_along(strips_south, "lat", -1)

    rest, lit = rest_features(state, surface, slots)
    five = layer_five.T
    five_first = five[2 * levels : 4 * levels]
    five_second = five[4 * levels : 6 * levels]
    five_winds = jnp.concatenate([five[: 2 * levels], five[6 * levels :]], axis=0)

    inner_out = inner(state, from_north, from_south)
    ozone_relay = relay(row_offset, ozone, ozone_near)
    ozone_far = shifted(ozone_relay, "lon", 2)
    winds, upwind, hidden, first = network(
        inner_out,
        (strips, strips_from_north, strips_from_south),
        rest,
        layers,
        five_first,
        lit,
        flat,
    )
    first_near = shifted(first, "lon", 1)
    other = second(5 * levels, hidden, five_second, lit, flat)
    other_near = shifted(other, "lon", 1)
    first_relay = relay(row_offset, first, first_near)
    first_far = shifted(first_relay, "lon", 2)
    other_relay = relay(row_offset, other, other_near)
    other_far = shifted(other_relay, "lon", 2)
    whole, flux, stay, come = winds_out(hidden, five_winds, lit, winds, upwind, fields)
    whole = advect(
        fields - 1, row_offset, ozone, ozone_near, ozone_far, stay, come, whole
    )
    whole = advect(3, row_offset, first, first_near, first_far, stay, come, whole)
    whole = advect(5, row_offset, other, other_near, other_far, stay, come, whole)
    return whole.reshape(fields, levels, rows, cols), flux


def solution(mesh):
    in_specs = (
        P(None, None, "lat", "lon"),
        P(None, "lat", "lon"),
        P(),
        P(),
        P(),
        P(),
        P(),
        P("lat", "lon", None),
        P("lat"),
    )
    out_specs = (P(None, None, "lat", "lon"), P(None, "lat", "lon"))
    return jax.shard_map(
        on_device, mesh=mesh, in_specs=in_specs, out_specs=out_specs, check_vma=False
    )
```

```python
import functools

import jax
import jax.numpy as jnp
from jax import lax
from jax.experimental import pallas as pl
from jax.experimental.pallas import tpu as pltpu
from jax.sharding import PartitionSpec as P


SUBSTEPS = 4
SOUND_COURANT = 0.6
PHYSICS_STEP = 0.5
LEAK_SLOPE = 0.15

STRIP = 6 * SUBSTEPS
F32 = jnp.float32
BF16 = jnp.bfloat16


def vmem():
    return pl.BlockSpec(memory_space=pltpu.VMEM)


def any_space():
    return pl.BlockSpec(memory_space=pl.ANY)


def params(mib):
    return pltpu.CompilerParams(vmem_limit_bytes=mib << 20)


def cost(flops, nbytes):
    return pl.CostEstimate(flops=flops, bytes_accessed=nbytes, transcendentals=0)


def iota(shape, dim):
    return lax.broadcasted_iota(jnp.int32, shape, dim)


def back(shift, size):
    return (size - shift) % size


def paired(tiles, rows, low):
    tiles = tiles.reshape((tiles.shape[0] // 2, 2) + tiles.shape[1:])
    even = tiles[:, 0]
    odd = pltpu.roll(tiles[:, 1], rows // 2, 1)
    return jnp.where(low, even, odd), jnp.where(low, odd, even)


def halo_rows(north_pair, south_pair, low):
    even = jnp.where(low, north_pair, south_pair)
    odd = pltpu.roll(jnp.where(low, south_pair, north_pair), north_pair.shape[-2] // 2, 1)
    return jnp.stack([even, odd], axis=1).reshape((-1,) + even.shape[1:])


def side_packs(tiles, lane):
    per = tiles.shape[-1] // STRIP
    west_packs, east_packs = [], []
    for pack in range(tiles.shape[0] // per):
        west = jnp.zeros(tiles.shape[1:], F32)
        east = jnp.zeros(tiles.shape[1:], F32)
        for slot in range(per):
            tile = tiles[pack * per + slot]
            start = slot * STRIP
            inside = (lane >= start) & (lane < start + STRIP)
            west = jnp.where(inside, pltpu.roll(tile, start + 2 * SUBSTEPS, 1), west)
            east = jnp.where(inside, pltpu.roll(tile, start + 4 * SUBSTEPS, 1), east)
        west_packs.append(west)
        east_packs.append(east)
    return jnp.stack(west_packs), jnp.stack(east_packs)


def tall(tiles):
    count, rows, cols = tiles.shape
    return tiles.reshape(count // 2, 2 * rows, cols).astype(BF16)


def messages_kernel(winds_ref, south_ref, north_ref, west_ref, east_ref):
    fields, levels, rows, cols = winds_ref.shape
    low = iota((rows, cols), 0) < rows // 2
    lane = iota((rows, cols), 1)
    held = winds_ref.reshape(fields * levels, rows, cols)

    def body(step, carry):
        tiles = held[pl.ds(step * 20, 20)]
        south, north = paired(tiles, rows, low)
        south_ref[pl.ds(step * 5, 5)] = tall(south)
        north_ref[pl.ds(step * 5, 5)] = tall(north)
        west, east = side_packs(tiles, lane)
        west_ref[pl.ds(step * 2, 2)] = tall(west)
        east_ref[pl.ds(step * 2, 2)] = tall(east)
        return carry

    steps = fields * levels // 20
    lax.fori_loop(0, steps, body, 0, unroll=steps)


def messages(winds):
    fields, levels, rows, cols = winds.shape

    def shape(count):
        return jax.ShapeDtypeStruct((count // 2, 2 * rows, cols), BF16)

    packs = fields * levels // (cols // STRIP)
    return pl.pallas_call(
        messages_kernel,
        out_shape=(shape(fields * levels // 2),) * 2 + (shape(packs),) * 2,
        in_specs=[vmem()],
        out_specs=(vmem(),) * 4,
        compiler_params=params(4),
        cost_estimate=cost(1 << 20, 2 << 20),
    )(winds)


def short(ref, at, size):
    rows, cols = ref.shape[1] // 2, ref.shape[2]
    return ref[pl.ds(at // 2, size // 2)].astype(F32).reshape(size, rows, cols)


def strips_kernel(own_west_ref, own_east_ref, from_east_ref, from_west_ref, out_ref, south_ref, north_ref):
    count = 2 * own_west_ref.shape[0]
    rows, cols = own_west_ref.shape[1] // 2, own_west_ref.shape[2]
    place = iota((rows, cols), 1) % STRIP
    low = iota((rows, cols), 0) < rows // 2
    value = short(own_east_ref, 0, count)
    value = jnp.where(place < 4 * SUBSTEPS, short(from_west_ref, 0, count), value)
    value = jnp.where(place < 3 * SUBSTEPS, short(from_east_ref, 0, count), value)
    value = jnp.where(place < 2 * SUBSTEPS, short(own_west_ref, 0, count), value)
    out_ref[...] = value
    south, north = paired(value, rows, low)
    south_ref[...] = tall(south)
    north_ref[...] = tall(north)


def strips_of(own_west, own_east, from_east, from_west):
    count, height, cols = own_west.shape
    half = jax.ShapeDtypeStruct((count // 2, height, cols), BF16)
    return pl.pallas_call(
        strips_kernel,
        out_shape=(jax.ShapeDtypeStruct((2 * count, height // 2, cols), F32), half, half),
        in_specs=[vmem()] * 4,
        out_specs=(vmem(),) * 3,
        compiler_params=params(4),
        cost_estimate=cost(1 << 20, 1 << 20),
    )(own_west, own_east, from_east, from_west)


def open_rows(rows, cols):
    place = iota((2 * rows, cols), 0)
    offset = jnp.where(place < rows + rows // 2, place, place - 2 * rows)
    row = lax.axis_index("lat") * rows + offset
    last = rows * lax.axis_size("lat") - 1
    return jnp.where((row >= 0) & (row < last), 1.0, 0.0).astype(F32)


def substeps(zonal, merid, press, free):
    rows, cols = zonal.shape[-2:]
    for _ in range(SUBSTEPS):
        zonal = zonal - SOUND_COURANT * (pltpu.roll(press, cols - 1, 2) - press)
        merid = (merid - SOUND_COURANT * (pltpu.roll(press, rows - 1, 1) - press)) * free
        press = press - SOUND_COURANT * (
            zonal - pltpu.roll(zonal, 1, 2) + merid - pltpu.roll(merid, 1, 1)
        )
    return zonal, merid, press


def inner_kernel(state_ref, from_north_ref, from_south_ref, out_ref):
    levels = state_ref.shape[1]
    rows, cols = state_ref.shape[2:]
    low = iota((rows, cols), 0) < rows // 2
    free = open_rows(rows, cols)
    parts = []
    for field in range(3):
        at = pl.ds(field * (levels // 4), levels // 4)
        north = from_north_ref[at].astype(F32).reshape(levels // 2, rows, cols)
        south = from_south_ref[at].astype(F32).reshape(levels // 2, rows, cols)
        side = halo_rows(north, south, low)
        parts.append(jnp.concatenate([state_ref[field], side], axis=1))
    for field, value in enumerate(substeps(*parts, free)):
        out_ref[field] = value[:, :rows]


def inner(state, from_north, from_south):
    _, levels, rows, cols = state.shape
    return pl.pallas_call(
        inner_kernel,
        out_shape=jax.ShapeDtypeStruct((3, levels, rows, cols), F32),
        in_specs=[vmem()] * 3,
        out_specs=vmem(),
        compiler_params=params(16),
        cost_estimate=cost(1 << 24, 4 << 20),
    )(state, from_north, from_south)


def rest_kernel(state_ref, surface_ref, slots_ref, rest_ref, lit_ref, ozone_ref, buffer, wide):
    fields, levels, rows, cols = state_ref.shape
    ozone_ref[...] = tall(state_ref[fields - 1])
    extra = surface_ref.shape[0]
    first = 3 * levels
    wide[...] = surface_ref[...].astype(F32).reshape(extra * rows, cols)
    flat = state_ref.reshape(fields * levels * rows, cols)
    buffer[0:first] = jnp.zeros((first, cols), F32)
    for row in range(rows):
        buffer[first : fields * levels] = flat[
            pl.ds(first * rows + row, (fields - 3) * levels, stride=rows), :
        ]
        buffer[fields * levels : fields * levels + extra] = wide[pl.ds(row, extra, stride=rows), :]
        rest_ref[:, row * cols : (row + 1) * cols] = buffer[...].astype(BF16)
    slots = slots_ref[...]
    count = slots.shape[1]
    in_row = (slots // cols == iota((rows, count), 0)).astype(F32).astype(BF16)
    in_col = (slots % cols == iota((cols, count), 0)).astype(F32).astype(BF16)
    lit_ref[...] = lax.dot_general(
        in_row, in_col, (((1,), (1,)), ((), ())), preferred_element_type=F32
    )


def rest_features(state, surface, slots):
    fields, levels, rows, cols = state.shape
    count = fields * levels + surface.shape[0]
    return pl.pallas_call(
        rest_kernel,
        out_shape=(
            jax.ShapeDtypeStruct((count, rows * cols), BF16),
            jax.ShapeDtypeStruct((rows, cols), F32),
            jax.ShapeDtypeStruct((levels // 2, 2 * rows, cols), BF16),
        ),
        in_specs=[vmem()] * 3,
        out_specs=(vmem(),) * 3,
        scratch_shapes=[
            pltpu.VMEM((count, cols), F32),
            pltpu.VMEM((surface.shape[0] * rows, cols), F32),
        ],
        compiler_params=params(12),
        cost_estimate=cost(1 << 24, 4 << 20),
    )(state, surface, slots)


def leaky(value):
    return jnp.maximum(value, LEAK_SLOPE * value).astype(BF16)


def tracer_update(weight, hidden, lit, state_at, out_ref, spread):
    rows, cols = lit.shape
    levels = weight.shape[0]
    result = lax.dot_general(
        weight, hidden, (((1,), (1,)), ((), ())), preferred_element_type=F32
    )
    for row in range(rows):
        spread[pl.ds(row, levels, stride=rows), :] = result[:, row * cols : (row + 1) * cols]

    def body(step, carry):
        value = spread[pl.ds(step * 10 * rows, 10 * rows), :].reshape(10, rows, cols)
        value = jnp.where(lit > 0.5, value.astype(BF16).astype(F32), 0.0)
        value = state_at(step) + PHYSICS_STEP * value
        out_ref[pl.ds(step * 5, 5)] = value.reshape(5, 2 * rows, cols).astype(BF16)
        return carry

    lax.fori_loop(0, levels // 10, body, 0)


def network_kernel(
    parts_count,
    inner_ref,
    here_ref,
    north_ref,
    south_ref,
    rest_ref,
    one_ref,
    two_ref,
    three_ref,
    four_ref,
    five_ref,
    lit_ref,
    state_ref,
    winds_ref,
    upwind_ref,
    hidden_ref,
    tracer_ref,
    strips,
    spread,
    features,
):
    _, levels, rows, cols = inner_ref.shape
    per = cols // STRIP
    packs = levels // per
    low = iota((rows, cols), 0) < rows // 2
    free = open_rows(rows, cols)
    parts = []
    for field in range(3):
        half = [short(ref, field * packs // 2, packs // 2) for ref in (north_ref, south_ref)]
        here = here_ref[pl.ds(field * packs, packs)]
        parts.append(jnp.concatenate([here, halo_rows(*half, low)], axis=1))
    for field, value in enumerate(substeps(*parts, free)):
        strips[field] = value[:, :rows]
    lane = iota((rows, cols), 1)

    def merge(step, carry):
        for slot in range(per):
            level = step * per + slot
            for field in range(3):
                strip = strips[field, step]
                west = pltpu.roll(strip, back(slot * STRIP + 4 * SUBSTEPS, cols), 1)
                east = pltpu.roll(strip, back(slot * STRIP + 2 * SUBSTEPS, cols), 1)
                value = inner_ref[field, level]
                value = jnp.where(lane < SUBSTEPS, west, value)
                value = jnp.where(lane >= cols - SUBSTEPS, east, value)
                winds_ref[pl.ds((field * levels + level) * rows, rows), :] = value
                if field == 0:
                    upwind_ref[level] = pltpu.roll(jnp.where(lane == cols - 1, west, value), 1, 1)
        return carry

    lax.fori_loop(0, packs, merge, 0, unroll=4)
    count = 3 * levels
    features[...] = rest_ref[...]
    for row in range(rows):
        features[0:count, row * cols : (row + 1) * cols] = winds_ref[
            pl.ds(row, count, stride=rows), :
        ].astype(BF16)
    total = rows * cols
    chunk = total // parts_count

    for part in range(parts_count):
        at = part * chunk
        hidden = leaky(
            lax.dot_general(
                features[:, at : at + chunk],
                one_ref[...],
                (((0,), (0,)), ((), ())),
                preferred_element_type=F32,
            )
        )
        for weight in (two_ref, three_ref, four_ref):
            hidden = leaky(jnp.dot(hidden, weight[...], preferred_element_type=F32))
        hidden_ref[at : at + chunk] = hidden
    tracer_update(
        five_ref[...],
        hidden_ref[...],
        lit_ref[...],
        lambda step: state_ref[pl.ds(3 * levels + step * 10, 10)],
        tracer_ref,
        spread,
    )


def network(inner_out, strips, rest, layers, five, lit, tracers, parts_count=2):
    _, levels, rows, cols = inner_out.shape
    count = five.shape[0]
    width = layers[3].shape[1]
    return pl.pallas_call(
        functools.partial(network_kernel, parts_count),
        out_shape=(
            jax.ShapeDtypeStruct((3 * levels * rows, cols), F32),
            jax.ShapeDtypeStruct((levels, rows, cols), F32),
            jax.ShapeDtypeStruct((rows * cols, width), BF16),
            jax.ShapeDtypeStruct((count // 2, 2 * rows, cols), BF16),
        ),
        in_specs=[vmem()] * 12,
        out_specs=(vmem(),) * 4,
        scratch_shapes=[
            pltpu.VMEM((3, levels * STRIP // (cols - cols % STRIP), rows, cols), F32),
            pltpu.VMEM((count * rows, cols), F32),
            pltpu.VMEM(rest.shape, BF16),
        ],
        compiler_params=params(32),
        cost_estimate=cost(4 << 30, 8 << 20),
    )(inner_out, *strips, rest, *layers, five, lit, tracers)


def second_kernel(start, hidden_ref, five_ref, lit_ref, state_ref, tracer_ref, spread):
    tracer_update(
        five_ref[...],
        hidden_ref[...],
        lit_ref[...],
        lambda step: state_ref[pl.ds(start + step * 10, 10)],
        tracer_ref,
        spread,
    )


def second(start, hidden, five, lit, tracers):
    rows, cols = lit.shape
    count = five.shape[0]
    return pl.pallas_call(
        functools.partial(second_kernel, start),
        out_shape=jax.ShapeDtypeStruct((count // 2, 2 * rows, cols), BF16),
        in_specs=[vmem()] * 4,
        out_specs=vmem(),
        scratch_shapes=[pltpu.VMEM((count * rows, cols), F32)],
        compiler_params=params(16),
        cost_estimate=cost(1 << 28, 3 << 20),
    )(hidden, five, lit, tracers)


def winds_kernel(
    hidden_ref, five_ref, lit_ref, winds_ref, upwind_ref, out_ref, flux_ref, stay_ref, come_ref,
    spread, updated, sem
):
    rows, cols = lit_ref.shape
    levels = upwind_ref.shape[0]
    fluxes = flux_ref.shape[0]
    result = lax.dot_general(
        five_ref[...], hidden_ref[...], (((1,), (1,)), ((), ())), preferred_element_type=F32
    )
    count = five_ref.shape[0]
    for row in range(rows):
        spread[pl.ds(row, count, stride=rows), :] = result[:, row * cols : (row + 1) * cols]
    lit = lit_ref[...] > 0.5

    def body(step, carry):
        value = spread[pl.ds(step * 10 * rows, 10 * rows), :].reshape(10, rows, cols)
        value = jnp.where(lit, value.astype(BF16).astype(F32), 0.0)
        wind = winds_ref[pl.ds(step * 10 * rows, 10 * rows), :].reshape(10, rows, cols)
        updated[pl.ds(step * 10, 10)] = wind + PHYSICS_STEP * value
        return carry

    lax.fori_loop(0, 2 * levels // 10, body, 0)
    updated[2 * levels : 3 * levels] = winds_ref[2 * levels * rows :, :].reshape(
        levels, rows, cols
    )
    copy = pltpu.make_async_copy(
        updated, out_ref.at[pl.ds(0, 3 * levels)], sem
    )
    copy.start()
    value = spread[2 * levels * rows :, :].reshape(fluxes, rows, cols)
    flux_ref[...] = jnp.where(lit, value, 0.0).astype(BF16)

    def share(step, carry):
        here = winds_ref[pl.ds(step * 10 * rows, 10 * rows), :].reshape(10, rows, cols)
        stay_ref[pl.ds(step * 10, 10)] = 0.5 - 0.45 * jnp.tanh(here)
        come_ref[pl.ds(step * 10, 10)] = 0.5 + 0.45 * jnp.tanh(upwind_ref[pl.ds(step * 10, 10)])
        return carry

    lax.fori_loop(0, levels // 10, share, 0)
    copy.wait()


def winds_out(hidden, five, lit, winds, upwind, fields):
    levels, rows, cols = upwind.shape
    fluxes = five.shape[0] - 2 * levels
    share = jax.ShapeDtypeStruct((levels, rows, cols), F32)
    return pl.pallas_call(
        winds_kernel,
        out_shape=(
            jax.ShapeDtypeStruct((fields * levels, rows, cols), F32),
            jax.ShapeDtypeStruct((fluxes, rows, cols), BF16),
            share,
            share,
        ),
        in_specs=[vmem()] * 5,
        out_specs=(any_space(), vmem(), vmem(), vmem()),
        scratch_shapes=[
            pltpu.VMEM((five.shape[0] * rows, cols), F32),
            pltpu.VMEM((3 * levels, rows, cols), F32),
            pltpu.SemaphoreType.DMA,
        ],
        compiler_params=params(16),
        cost_estimate=cost(1 << 28, 4 << 20),
    )(hidden, five, lit, winds, upwind)


def spread_offsets(offset_ref, rows, cols):
    place = iota((rows, cols), 0)
    offset = jnp.zeros((rows, cols), jnp.int32)
    for row in range(rows):
        offset = jnp.where(place == row, offset_ref[row], offset)
    return offset // cols, offset % cols


def along(value, index):
    return jnp.take_along_axis(value, index, axis=1, mode="promise_in_bounds")


def relay_kernel(offset_ref, own_ref, near_ref, out_ref):
    rows = own_ref.shape[1] // 2
    cols = own_ref.shape[2]
    pairs = own_ref.shape[0]
    blocks, cells = spread_offsets(offset_ref, rows, cols)
    lane = iota((rows, cols), 1)
    take_near = (blocks >= 2) & (lane > cols - 1 - cells)
    edge = cols - 1 - cells

    def body(step, column):
        at = pl.ds(step * 10, 10)
        own = own_ref[at].astype(F32).reshape(20, rows, cols)
        near = near_ref[at].astype(F32).reshape(20, rows, cols)
        out_ref[at] = tall(jnp.where(take_near, near, own))
        for level in range(20):
            column = jnp.where(lane == step * 20 + level, along(near[level], edge), column)
        return column

    steps = pairs // 10
    column = lax.fori_loop(0, steps, body, jnp.zeros((rows, cols), F32), unroll=3)
    out_ref[pairs] = jnp.concatenate([column, column], axis=0).astype(BF16)


def relay(offset, own, near):
    pairs, height, cols = own.shape
    return pl.pallas_call(
        relay_kernel,
        out_shape=jax.ShapeDtypeStruct((pairs + 1, height, cols), BF16),
        in_specs=[pl.BlockSpec(memory_space=pltpu.SMEM), vmem(), vmem()],
        out_specs=vmem(),
        compiler_params=params(8),
        cost_estimate=cost(1 << 20, 1 << 20),
    )(offset, own, near)


def advect_kernel(
    first, group, offset_ref, own_ref, near_ref, far_ref, stay_ref, come_ref, whole_ref, out_ref, result, sem
):
    levels, rows, cols = stay_ref.shape
    pairs = own_ref.shape[0]
    blocks, cells = spread_offsets(offset_ref, rows, cols)
    lane = iota((rows, cols), 1)
    from_right = lane <= cols - 1 - cells
    index = (lane - cells) & (cols - 1)
    column = far_ref[pairs].astype(F32)[:rows]
    is_zero, is_one, is_two = blocks == 0, blocks == 1, blocks >= 2
    steps = levels // group
    edge_index = cols - 1 - cells

    def body(step, carry):
        at = pl.ds(step * (group // 2), group // 2)
        share = pl.ds(lax.rem(step, steps) * group, group)
        own = own_ref[at].astype(F32).reshape(group, rows, cols)
        near = near_ref[at].astype(F32).reshape(group, rows, cols)
        far = far_ref[at].astype(F32).reshape(group, rows, cols)
        stay = stay_ref[share]
        come = come_ref[share]
        right = jnp.where(is_zero, own, jnp.where(is_one, near, far))
        left = jnp.where(is_zero, near, far)
        merged = jnp.where(from_right, right, left)
        edges = jnp.where(is_two, column, left)
        for level in range(group):
            which = jnp.where(is_two, step * group + level, edge_index)
            here = along(merged[level], index)
            behind = jnp.where(lane == 0, along(edges[level], which), pltpu.roll(here, 1, 1))
            result[step * group + level] = stay[level] * here + come[level] * behind
        copy_of(step).start()
        return carry

    def copy_of(step):
        return pltpu.make_async_copy(
            result.at[pl.ds(step * group, group)],
            out_ref.at[pl.ds(first * levels + step * group, group)],
            sem.at[step],
        )

    count = 2 * pairs // group
    lax.fori_loop(0, count, body, 0)
    for step in range(count):
        copy_of(step).wait()


def advect(first, offset, own, near, far, stay, come, whole, group=30):
    pairs, height, cols = own.shape
    return pl.pallas_call(
        functools.partial(advect_kernel, first, group),
        out_shape=jax.ShapeDtypeStruct(whole.shape, F32),
        in_specs=[pl.BlockSpec(memory_space=pltpu.SMEM)] + [vmem()] * 5 + [any_space()],
        out_specs=any_space(),
        scratch_shapes=[
            pltpu.VMEM((2 * pairs, height // 2, cols), F32),
            pltpu.SemaphoreType.DMA((2 * pairs // group,)),
        ],
        input_output_aliases={6: 0},
        compiler_params=params(12),
        cost_estimate=cost(1 << 22, 3 << 20),
    )(offset, own, near, far, stay, come, whole)


def shifted(value, axis, steps):
    count = lax.axis_size(axis)
    return lax.ppermute(value, axis, [(i, (i + steps) % count) for i in range(count)])


def passed_along(block, axis, distance):
    devices = range(lax.axis_size(axis))
    return lax.ppermute(
        block, axis, [(i, i + distance) for i in devices if i + distance in devices]
    )


def on_device(
    state,
    surface,
    layer_one,
    layer_two,
    layer_three,
    layer_four,
    layer_five,
    lit_columns,
    row_offset,
):
    return tile_step(
        state,
        surface,
        (layer_one, layer_two, layer_three, layer_four),
        layer_five,
        lit_columns,
        row_offset,
    )


def tile_step(state, surface, layers, layer_five, lit_columns, row_offset):
    fields, levels, rows, cols = state.shape
    slots = lit_columns.reshape(1, rows * cols)
    flat = state.reshape(fields * levels, rows, cols)

    start_winds = state[:3]
    to_south, to_north, to_west, to_east = messages(start_winds)
    rest, lit, ozone = rest_features(state, surface, slots)
    from_east = shifted(to_west, "lon", -1)
    from_west = shifted(to_east, "lon", 1)
    from_south = shifted(to_north, "lat", 1)
    from_north = passed_along(to_south, "lat", -1)
    ozone_near = shifted(ozone, "lon", 1)
    strips, strips_south, strips_north = strips_of(to_west, to_east, from_east, from_west)
    strips_from_south = shifted(strips_north, "lat", 1)
    strips_from_north = passed_along(strips_south, "lat", -1)

    five = layer_five.T
    five_first = five[2 * levels : 4 * levels]
    five_second = five[4 * levels : 6 * levels]
    five_winds = jnp.concatenate([five[: 2 * levels], five[6 * levels :]], axis=0)

    inner_out = inner(start_winds, from_north, from_south)
    ozone_relay = relay(row_offset, ozone, ozone_near)
    ozone_far = shifted(ozone_relay, "lon", 2)
    winds, upwind, hidden, first = network(
        inner_out,
        (strips, strips_from_north, strips_from_south),
        rest,
        layers,
        five_first,
        lit,
        flat,
    )
    first_near = shifted(first, "lon", 1)
    other = second(5 * levels, hidden, five_second, lit, flat)
    other_near = shifted(other, "lon", 1)
    first_relay = relay(row_offset, first, first_near)
    first_far = shifted(first_relay, "lon", 2)
    other_relay = relay(row_offset, other, other_near)
    other_far = shifted(other_relay, "lon", 2)
    whole, flux, stay, come = winds_out(hidden, five_winds, lit, winds, upwind, fields)
    whole = advect(
        fields - 1, row_offset, ozone, ozone_near, ozone_far, stay, come, whole
    )
    whole = advect(3, row_offset, first, first_near, first_far, stay, come, whole)
    whole = advect(5, row_offset, other, other_near, other_far, stay, come, whole)
    return whole.reshape(fields, levels, rows, cols), flux


def solution(mesh):
    in_specs = (
        P(None, None, "lat", "lon"),
        P(None, "lat", "lon"),
        P(),
        P(),
        P(),
        P(),
        P(),
        P("lat", "lon", None),
        P("lat"),
    )
    out_specs = (P(None, None, "lat", "lon"), P(None, "lat", "lon"))
    return jax.shard_map(
        on_device, mesh=mesh, in_specs=in_specs, out_specs=out_specs, check_vma=False
    )
```

```python
import functools

import jax
import jax.numpy as jnp
from jax import lax
from jax.experimental import pallas as pl
from jax.experimental.pallas import tpu as pltpu
from jax.sharding import PartitionSpec as P


SUBSTEPS = 4
SOUND_COURANT = 0.6
PHYSICS_STEP = 0.5
LEAK_SLOPE = 0.15

STRIP = 6 * SUBSTEPS
F32 = jnp.float32
BF16 = jnp.bfloat16


def vmem():
    return pl.BlockSpec(memory_space=pltpu.VMEM)


def any_space():
    return pl.BlockSpec(memory_space=pl.ANY)


def params(mib):
    return pltpu.CompilerParams(vmem_limit_bytes=mib << 20)


def cost(flops, nbytes):
    return pl.CostEstimate(flops=flops, bytes_accessed=nbytes, transcendentals=0)


def iota(shape, dim):
    return lax.broadcasted_iota(jnp.int32, shape, dim)


def back(shift, size):
    return (size - shift) % size


def paired(tiles, rows, low):
    tiles = tiles.reshape((tiles.shape[0] // 2, 2) + tiles.shape[1:])
    even = tiles[:, 0]
    odd = pltpu.roll(tiles[:, 1], rows // 2, 1)
    return jnp.where(low, even, odd), jnp.where(low, odd, even)


def halo_rows(north_pair, south_pair, low):
    even = jnp.where(low, north_pair, south_pair)
    odd = pltpu.roll(jnp.where(low, south_pair, north_pair), north_pair.shape[-2] // 2, 1)
    return jnp.stack([even, odd], axis=1).reshape((-1,) + even.shape[1:])


def side_packs(tiles, lane):
    per = tiles.shape[-1] // STRIP
    west_packs, east_packs = [], []
    for pack in range(tiles.shape[0] // per):
        west = jnp.zeros(tiles.shape[1:], F32)
        east = jnp.zeros(tiles.shape[1:], F32)
        for slot in range(per):
            tile = tiles[pack * per + slot]
            start = slot * STRIP
            inside = (lane >= start) & (lane < start + STRIP)
            west = jnp.where(inside, pltpu.roll(tile, start + 2 * SUBSTEPS, 1), west)
            east = jnp.where(inside, pltpu.roll(tile, start + 4 * SUBSTEPS, 1), east)
        west_packs.append(west)
        east_packs.append(east)
    return jnp.stack(west_packs), jnp.stack(east_packs)


def tall(tiles):
    count, rows, cols = tiles.shape
    return tiles.reshape(count // 2, 2 * rows, cols).astype(BF16)


def messages_kernel(winds_ref, south_ref, north_ref, west_ref, east_ref):
    fields, levels, rows, cols = winds_ref.shape
    low = iota((rows, cols), 0) < rows // 2
    lane = iota((rows, cols), 1)
    held = winds_ref.reshape(fields * levels, rows, cols)

    def body(step, carry):
        tiles = held[pl.ds(step * 20, 20)]
        south, north = paired(tiles, rows, low)
        south_ref[pl.ds(step * 5, 5)] = tall(south)
        north_ref[pl.ds(step * 5, 5)] = tall(north)
        west, east = side_packs(tiles, lane)
        west_ref[pl.ds(step * 2, 2)] = tall(west)
        east_ref[pl.ds(step * 2, 2)] = tall(east)
        return carry

    steps = fields * levels // 20
    lax.fori_loop(0, steps, body, 0, unroll=steps)


def messages(winds):
    fields, levels, rows, cols = winds.shape

    def shape(count):
        return jax.ShapeDtypeStruct((count // 2, 2 * rows, cols), BF16)

    packs = fields * levels // (cols // STRIP)
    return pl.pallas_call(
        messages_kernel,
        out_shape=(shape(fields * levels // 2),) * 2 + (shape(packs),) * 2,
        in_specs=[vmem()],
        out_specs=(vmem(),) * 4,
        compiler_params=params(4),
        cost_estimate=cost(1 << 20, 2 << 20),
    )(winds)


def short(ref, at, size):
    rows, cols = ref.shape[1] // 2, ref.shape[2]
    return ref[pl.ds(at // 2, size // 2)].astype(F32).reshape(size, rows, cols)


def strips_kernel(own_west_ref, own_east_ref, from_east_ref, from_west_ref, out_ref, south_ref, north_ref):
    count = 2 * own_west_ref.shape[0]
    rows, cols = own_west_ref.shape[1] // 2, own_west_ref.shape[2]
    place = iota((rows, cols), 1) % STRIP
    low = iota((rows, cols), 0) < rows // 2
    value = short(own_east_ref, 0, count)
    value = jnp.where(place < 4 * SUBSTEPS, short(from_west_ref, 0, count), value)
    value = jnp.where(place < 3 * SUBSTEPS, short(from_east_ref, 0, count), value)
    value = jnp.where(place < 2 * SUBSTEPS, short(own_west_ref, 0, count), value)
    out_ref[...] = value
    south, north = paired(value, rows, low)
    south_ref[...] = tall(south)
    north_ref[...] = tall(north)


def strips_of(own_west, own_east, from_east, from_west):
    count, height, cols = own_west.shape
    half = jax.ShapeDtypeStruct((count // 2, height, cols), BF16)
    return pl.pallas_call(
        strips_kernel,
        out_shape=(jax.ShapeDtypeStruct((2 * count, height // 2, cols), F32), half, half),
        in_specs=[vmem()] * 4,
        out_specs=(vmem(),) * 3,
        compiler_params=params(4),
        cost_estimate=cost(1 << 20, 1 << 20),
    )(own_west, own_east, from_east, from_west)


def open_rows(rows, cols):
    place = iota((2 * rows, cols), 0)
    offset = jnp.where(place < rows + rows // 2, place, place - 2 * rows)
    row = lax.axis_index("lat") * rows + offset
    last = rows * lax.axis_size("lat") - 1
    return jnp.where((row >= 0) & (row < last), 1.0, 0.0).astype(F32)


def substeps(zonal, merid, press, free):
    rows, cols = zonal.shape[-2:]
    for _ in range(SUBSTEPS):
        zonal = zonal - SOUND_COURANT * (pltpu.roll(press, cols - 1, 2) - press)
        merid = (merid - SOUND_COURANT * (pltpu.roll(press, rows - 1, 1) - press)) * free
        press = press - SOUND_COURANT * (
            zonal - pltpu.roll(zonal, 1, 2) + merid - pltpu.roll(merid, 1, 1)
        )
    return zonal, merid, press


def inner_kernel(state_ref, from_north_ref, from_south_ref, out_ref):
    levels = state_ref.shape[1]
    rows, cols = state_ref.shape[2:]
    low = iota((rows, cols), 0) < rows // 2
    free = open_rows(rows, cols)
    parts = []
    for field in range(3):
        at = pl.ds(field * (levels // 4), levels // 4)
        north = from_north_ref[at].astype(F32).reshape(levels // 2, rows, cols)
        south = from_south_ref[at].astype(F32).reshape(levels // 2, rows, cols)
        side = halo_rows(north, south, low)
        parts.append(jnp.concatenate([state_ref[field], side], axis=1))
    for field, value in enumerate(substeps(*parts, free)):
        out_ref[field] = value[:, :rows]


def inner(state, from_north, from_south):
    _, levels, rows, cols = state.shape
    return pl.pallas_call(
        inner_kernel,
        out_shape=jax.ShapeDtypeStruct((3, levels, rows, cols), F32),
        in_specs=[vmem()] * 3,
        out_specs=vmem(),
        compiler_params=params(16),
        cost_estimate=cost(1 << 24, 4 << 20),
    )(state, from_north, from_south)


def rest_kernel(state_ref, surface_ref, slots_ref, rest_ref, lit_ref, ozone_ref, buffer, wide):
    fields, levels, rows, cols = state_ref.shape
    ozone_ref[...] = tall(state_ref[fields - 1])
    extra = surface_ref.shape[0]
    first = 3 * levels
    wide[...] = surface_ref[...].astype(F32).reshape(extra * rows, cols)
    flat = state_ref.reshape(fields * levels * rows, cols)
    buffer[0:first] = jnp.zeros((first, cols), F32)
    for row in range(rows):
        buffer[first : fields * levels] = flat[
            pl.ds(first * rows + row, (fields - 3) * levels, stride=rows), :
        ]
        buffer[fields * levels : fields * levels + extra] = wide[pl.ds(row, extra, stride=rows), :]
        rest_ref[:, row * cols : (row + 1) * cols] = buffer[...].astype(BF16)
    slots = slots_ref[...]
    count = slots.shape[1]
    in_row = (slots // cols == iota((rows, count), 0)).astype(F32).astype(BF16)
    in_col = (slots % cols == iota((cols, count), 0)).astype(F32).astype(BF16)
    lit_ref[...] = lax.dot_general(
        in_row, in_col, (((1,), (1,)), ((), ())), preferred_element_type=F32
    )


def rest_features(state, surface, slots):
    fields, levels, rows, cols = state.shape
    count = fields * levels + surface.shape[0]
    return pl.pallas_call(
        rest_kernel,
        out_shape=(
            jax.ShapeDtypeStruct((count, rows * cols), BF16),
            jax.ShapeDtypeStruct((rows, cols), F32),
            jax.ShapeDtypeStruct((levels // 2, 2 * rows, cols), BF16),
        ),
        in_specs=[vmem()] * 3,
        out_specs=(vmem(),) * 3,
        scratch_shapes=[
            pltpu.VMEM((count, cols), F32),
            pltpu.VMEM((surface.shape[0] * rows, cols), F32),
        ],
        compiler_params=params(12),
        cost_estimate=cost(1 << 24, 4 << 20),
    )(state, surface, slots)


def leaky(value):
    return jnp.maximum(value, LEAK_SLOPE * value).astype(BF16)


def half_tiles(tiles, low, north):
    rows = tiles.shape[1]
    tiles = tiles.reshape((tiles.shape[0] // 2, 2) + tiles.shape[1:])
    even, odd = tiles[:, 0], tiles[:, 1]
    if north:
        return jnp.where(low, pltpu.roll(even, rows // 2, 1), odd)
    return jnp.where(low, even, pltpu.roll(odd, rows // 2, 1))


def half_step(features_ref, layers, five_ref, lit_ref, state_ref, first, north, hidden_ref, tracer_ref, spread):
    rows, cols = lit_ref.shape
    half = rows // 2
    levels = five_ref.shape[0]
    low = iota((rows, cols), 0) < half
    at = half * cols if north else 0
    hidden = leaky(
        lax.dot_general(
            features_ref[:, at : at + half * cols],
            layers[0][...],
            (((0,), (0,)), ((), ())),
            preferred_element_type=F32,
        )
    )
    for weight in layers[1:]:
        hidden = leaky(jnp.dot(hidden, weight[...], preferred_element_type=F32))
    hidden_ref[...] = hidden
    result = lax.dot_general(
        five_ref[...], hidden, (((1,), (1,)), ((), ())), preferred_element_type=F32
    )
    for row in range(half):
        spread[pl.ds(row, levels, stride=half), :] = result[:, row * cols : (row + 1) * cols]
    lit = lit_ref[...]
    other = pltpu.roll(lit, half, 0)
    lit = jnp.where(low, other, lit) if north else jnp.where(low, lit, other)

    def body(step, carry):
        value = spread[pl.ds(step * 10 * rows, 10 * rows), :].reshape(10, rows, cols)
        value = jnp.where(lit > 0.5, value.astype(BF16).astype(F32), 0.0)
        held = half_tiles(state_ref[pl.ds(first + step * 20, 20)], low, north)
        tracer_ref[pl.ds(step * 5, 5)] = tall(held + PHYSICS_STEP * value)
        return carry

    lax.fori_loop(0, levels // 20, body, 0, unroll=3)


def network_kernel(
    inner_ref,
    here_ref,
    north_ref,
    south_ref,
    rest_ref,
    one_ref,
    two_ref,
    three_ref,
    four_ref,
    five_ref,
    lit_ref,
    state_ref,
    winds_ref,
    upwind_ref,
    features,
    hidden_ref,
    tracer_ref,
    strips,
    spread,
):
    _, levels, rows, cols = inner_ref.shape
    per = cols // STRIP
    packs = levels // per
    low = iota((rows, cols), 0) < rows // 2
    free = open_rows(rows, cols)
    parts = []
    for field in range(3):
        half = [short(ref, field * packs // 2, packs // 2) for ref in (north_ref, south_ref)]
        here = here_ref[pl.ds(field * packs, packs)]
        parts.append(jnp.concatenate([here, halo_rows(*half, low)], axis=1))
    for field, value in enumerate(substeps(*parts, free)):
        strips[field] = value[:, :rows]
    lane = iota((rows, cols), 1)

    def merge(step, carry):
        for slot in range(per):
            level = step * per + slot
            for field in range(3):
                strip = strips[field, step]
                west = pltpu.roll(strip, back(slot * STRIP + 4 * SUBSTEPS, cols), 1)
                east = pltpu.roll(strip, back(slot * STRIP + 2 * SUBSTEPS, cols), 1)
                value = inner_ref[field, level]
                value = jnp.where(lane < SUBSTEPS, west, value)
                value = jnp.where(lane >= cols - SUBSTEPS, east, value)
                winds_ref[pl.ds((field * levels + level) * rows, rows), :] = value
                if field == 0:
                    upwind_ref[level] = pltpu.roll(jnp.where(lane == cols - 1, west, value), 1, 1)
        return carry

    lax.fori_loop(0, packs, merge, 0, unroll=packs)
    count = 3 * levels
    features[...] = rest_ref[...]
    for row in range(rows):
        features[0:count, row * cols : (row + 1) * cols] = winds_ref[
            pl.ds(row, count, stride=rows), :
        ].astype(BF16)
    half_step(
        features,
        (one_ref, two_ref, three_ref, four_ref),
        five_ref,
        lit_ref,
        state_ref,
        3 * levels,
        False,
        hidden_ref,
        tracer_ref,
        spread,
    )


def network(inner_out, strips, rest, layers, five, lit, flat):
    _, levels, rows, cols = inner_out.shape
    count = five.shape[0]
    return pl.pallas_call(
        network_kernel,
        out_shape=(
            jax.ShapeDtypeStruct((3 * levels * rows, cols), F32),
            jax.ShapeDtypeStruct((levels, rows, cols), F32),
            jax.ShapeDtypeStruct(rest.shape, BF16),
            jax.ShapeDtypeStruct((rows * cols // 2, layers[3].shape[1]), BF16),
            jax.ShapeDtypeStruct((count // 4, 2 * rows, cols), BF16),
        ),
        in_specs=[vmem()] * 12,
        out_specs=(vmem(),) * 5,
        scratch_shapes=[
            pltpu.VMEM((3, levels * STRIP // (cols - cols % STRIP), rows, cols), F32),
            pltpu.VMEM((count * rows // 2, cols), F32),
        ],
        compiler_params=params(32),
        cost_estimate=cost(3 << 30, 8 << 20),
    )(inner_out, *strips, rest, *layers, five, lit, flat)


def second_kernel(
    first, features_ref, one_ref, two_ref, three_ref, four_ref, five_ref, lit_ref, state_ref,
    hidden_ref, tracer_ref, spread,
):
    layers = (one_ref, two_ref, three_ref, four_ref)
    half_step(
        features_ref, layers, five_ref, lit_ref, state_ref, first, True, hidden_ref, tracer_ref, spread
    )


def second(first, features, layers, five, lit, flat):
    rows, cols = lit.shape
    count = five.shape[0]
    return pl.pallas_call(
        functools.partial(second_kernel, first),
        out_shape=(
            jax.ShapeDtypeStruct((rows * cols // 2, layers[3].shape[1]), BF16),
            jax.ShapeDtypeStruct((count // 4, 2 * rows, cols), BF16),
        ),
        in_specs=[vmem()] * 8,
        out_specs=(vmem(),) * 2,
        scratch_shapes=[pltpu.VMEM((count * rows // 2, cols), F32)],
        compiler_params=params(24),
        cost_estimate=cost(2 << 30, 6 << 20),
    )(features, *layers, five, lit, flat)


def winds_kernel(
    south_ref, north_ref, five_ref, lit_ref, winds_ref, upwind_ref, out_ref, flux_ref,
    stay_ref, come_ref, stay_south_ref, come_south_ref, stay_north_ref, come_north_ref,
    spread, updated, sem
):
    rows, cols = lit_ref.shape
    levels = upwind_ref.shape[0]
    fluxes = flux_ref.shape[0]
    count = five_ref.shape[0]
    for side, hidden_ref in enumerate((south_ref, north_ref)):
        result = lax.dot_general(
            five_ref[...], hidden_ref[...], (((1,), (1,)), ((), ())), preferred_element_type=F32
        )
        for row in range(rows // 2):
            spread[pl.ds(side * (rows // 2) + row, count, stride=rows), :] = result[
                :, row * cols : (row + 1) * cols
            ]
    lit = lit_ref[...] > 0.5
    low = iota((rows, cols), 0) < rows // 2

    def body(step, carry):
        value = spread[pl.ds(step * 10 * rows, 10 * rows), :].reshape(10, rows, cols)
        value = jnp.where(lit, value.astype(BF16).astype(F32), 0.0)
        wind = winds_ref[pl.ds(step * 10 * rows, 10 * rows), :].reshape(10, rows, cols)
        updated[pl.ds(step * 10, 10)] = wind + PHYSICS_STEP * value
        return carry

    lax.fori_loop(0, 2 * levels // 10, body, 0)
    updated[2 * levels : 3 * levels] = winds_ref[2 * levels * rows :, :].reshape(
        levels, rows, cols
    )
    copy = pltpu.make_async_copy(
        updated, out_ref.at[pl.ds(0, 3 * levels)], sem
    )
    copy.start()
    value = spread[2 * levels * rows :, :].reshape(fluxes, rows, cols)
    flux_ref[...] = jnp.where(lit, value, 0.0).astype(BF16)

    def share(step, carry):
        here = winds_ref[pl.ds(step * 10 * rows, 10 * rows), :].reshape(10, rows, cols)
        stay = 0.5 - 0.45 * jnp.tanh(here)
        come = 0.5 + 0.45 * jnp.tanh(upwind_ref[pl.ds(step * 10, 10)])
        stay_ref[pl.ds(step * 10, 10)] = stay
        come_ref[pl.ds(step * 10, 10)] = come
        stay_south_ref[pl.ds(step * 5, 5)] = half_tiles(stay, low, False)
        come_south_ref[pl.ds(step * 5, 5)] = half_tiles(come, low, False)
        stay_north_ref[pl.ds(step * 5, 5)] = half_tiles(stay, low, True)
        come_north_ref[pl.ds(step * 5, 5)] = half_tiles(come, low, True)
        return carry

    lax.fori_loop(0, levels // 10, share, 0)
    copy.wait()


def winds_out(hidden_south, hidden_north, five, lit, winds, upwind, fields):
    levels, rows, cols = upwind.shape
    fluxes = five.shape[0] - 2 * levels
    share = jax.ShapeDtypeStruct((levels, rows, cols), F32)
    part = jax.ShapeDtypeStruct((levels // 2, rows, cols), F32)
    return pl.pallas_call(
        winds_kernel,
        out_shape=(
            jax.ShapeDtypeStruct((fields * levels, rows, cols), F32),
            jax.ShapeDtypeStruct((fluxes, rows, cols), BF16),
            share,
            share,
            part,
            part,
            part,
            part,
        ),
        in_specs=[vmem()] * 6,
        out_specs=(any_space(),) + (vmem(),) * 7,
        scratch_shapes=[
            pltpu.VMEM((five.shape[0] * rows, cols), F32),
            pltpu.VMEM((3 * levels, rows, cols), F32),
            pltpu.SemaphoreType.DMA,
        ],
        compiler_params=params(16),
        cost_estimate=cost(1 << 28, 4 << 20),
    )(hidden_south, hidden_north, five, lit, winds, upwind)


def spread_offsets(offset_ref, shape, base, span):
    rows, cols = shape
    place = iota((rows, cols), 0) % span
    offset = jnp.zeros((rows, cols), jnp.int32)
    for row in range(span):
        offset = jnp.where(place == row, offset_ref[base + row], offset)
    return offset // cols, offset % cols


def along(value, index):
    return jnp.take_along_axis(value, index, axis=1, mode="promise_in_bounds")


def relay_kernel(base, span, offset_ref, own_ref, near_ref, out_ref):
    rows = own_ref.shape[1] // 2
    cols = own_ref.shape[2]
    pairs = own_ref.shape[0]
    blocks, cells = spread_offsets(offset_ref, (rows, cols), base, span)
    lane = iota((rows, cols), 1)
    take_near = (blocks >= 2) & (lane > cols - 1 - cells)
    edge = cols - 1 - cells

    def body(step, column):
        at = pl.ds(step * 10, 10)
        own = own_ref[at].astype(F32).reshape(20, rows, cols)
        near = near_ref[at].astype(F32).reshape(20, rows, cols)
        out_ref[at] = tall(jnp.where(take_near, near, own))
        for level in range(20):
            column = jnp.where(lane == step * 20 + level, along(near[level], edge), column)
        return column

    steps = pairs // 10
    column = lax.fori_loop(0, steps, body, jnp.zeros((rows, cols), F32), unroll=3)
    out_ref[pairs] = jnp.concatenate([column, column], axis=0).astype(BF16)


def relay(offset, own, near, base, span):
    pairs, height, cols = own.shape
    return pl.pallas_call(
        functools.partial(relay_kernel, base, span),
        out_shape=jax.ShapeDtypeStruct((pairs + 1, height, cols), BF16),
        in_specs=[pl.BlockSpec(memory_space=pltpu.SMEM), vmem(), vmem()],
        out_specs=vmem(),
        compiler_params=params(8),
        cost_estimate=cost(1 << 20, 1 << 20),
    )(offset, own, near)


def blend(offset_ref, shape, base, span):
    rows, cols = shape
    blocks, cells = spread_offsets(offset_ref, shape, base, span)
    lane = iota((rows, cols), 1)
    from_right = lane <= cols - 1 - cells
    index = (lane - cells) & (cols - 1)
    edge_index = cols - 1 - cells
    is_zero, is_one, is_two = blocks == 0, blocks == 1, blocks >= 2

    def tiles(own, near, far, column, stay, come, first):
        right = jnp.where(is_zero, own, jnp.where(is_one, near, far))
        left = jnp.where(is_zero, near, far)
        merged = jnp.where(from_right, right, left)
        edges = jnp.where(is_two, column, left)
        values = []
        for tile in range(own.shape[0]):
            which = jnp.where(is_two, first + tile, edge_index)
            here = along(merged[tile], index)
            behind = jnp.where(lane == 0, along(edges[tile], which), pltpu.roll(here, 1, 1))
            values.append(stay[tile] * here + come[tile] * behind)
        return values

    return tiles


def read_tiles(refs, step, group, shape):
    at = pl.ds(step * (group // 2), group // 2)
    return [ref[at].astype(F32).reshape((group,) + shape) for ref in refs]


def last_column(far_ref, pairs, rows):
    return far_ref[pairs].astype(F32)[:rows]


def advect_ozone_kernel(
    first, offset_ref, own_ref, near_ref, far_ref, stay_ref, come_ref, whole_ref, out_ref, result, sem
):
    levels, rows, cols = stay_ref.shape
    group = levels // 2
    tiles = blend(offset_ref, (rows, cols), 0, rows)
    column = last_column(far_ref, own_ref.shape[0], rows)
    copies = []
    for step in range(2):
        share = pl.ds(step * group, group)
        values = tiles(
            *read_tiles((own_ref, near_ref, far_ref), step, group, (rows, cols)),
            column,
            stay_ref[share],
            come_ref[share],
            step * group,
        )
        for tile, value in enumerate(values):
            result[step * group + tile] = value
        copy = pltpu.make_async_copy(
            result.at[share], out_ref.at[pl.ds(first * levels + step * group, group)], sem.at[step]
        )
        copy.start()
        copies.append(copy)
    for copy in copies:
        copy.wait()


def advect_ozone(first, offset, own, near, far, stay, come, whole):
    levels, rows, cols = stay.shape
    return pl.pallas_call(
        functools.partial(advect_ozone_kernel, first),
        out_shape=jax.ShapeDtypeStruct(whole.shape, F32),
        in_specs=[pl.BlockSpec(memory_space=pltpu.SMEM)] + [vmem()] * 5 + [any_space()],
        out_specs=any_space(),
        scratch_shapes=[pltpu.VMEM((levels, rows, cols), F32), pltpu.SemaphoreType.DMA((2,))],
        input_output_aliases={6: 0},
        compiler_params=params(8),
        cost_estimate=cost(1 << 22, 2 << 20),
    )(offset, own, near, far, stay, come, whole)


def advect_south_kernel(offset_ref, own_ref, near_ref, far_ref, stay_ref, come_ref, out_ref):
    group, rows, cols = stay_ref.shape
    pairs = own_ref.shape[0]
    tiles = blend(offset_ref, (rows, cols), 0, rows // 2)
    column = last_column(far_ref, pairs, rows)

    def body(step, carry):
        values = tiles(
            *read_tiles((own_ref, near_ref, far_ref), step, group, (rows, cols)),
            column,
            stay_ref[...],
            come_ref[...],
            step * group,
        )
        for tile, value in enumerate(values):
            out_ref[step * group + tile] = value
        return carry

    lax.fori_loop(0, 2 * pairs // group, body, 0)


def advect_south(offset, own, near, far, stay, come):
    pairs, height, cols = own.shape
    return pl.pallas_call(
        advect_south_kernel,
        out_shape=jax.ShapeDtypeStruct((2 * pairs, height // 2, cols), F32),
        in_specs=[pl.BlockSpec(memory_space=pltpu.SMEM)] + [vmem()] * 5,
        out_specs=vmem(),
        compiler_params=params(8),
        cost_estimate=cost(1 << 22, 2 << 20),
    )(offset, own, near, far, stay, come)


def advect_north_kernel(
    first, offset_ref, own_ref, near_ref, far_ref, stay_ref, come_ref, south_ref, whole_ref, out_ref,
    result, sem,
):
    group, rows, cols = stay_ref.shape
    pairs = own_ref.shape[0]
    tiles = blend(offset_ref, (rows, cols), rows // 2, rows // 2)
    column = last_column(far_ref, pairs, rows)
    low = iota((rows, cols), 0) < rows // 2
    count = 2 * pairs // group

    def copy_of(step):
        span = pl.ds(step * 2 * group, 2 * group)
        return pltpu.make_async_copy(
            result.at[span],
            out_ref.at[pl.ds((first + step) * 2 * group, 2 * group)],
            sem.at[step],
        )

    def body(step, carry):
        values = tiles(
            *read_tiles((own_ref, near_ref, far_ref), step, group, (rows, cols)),
            column,
            stay_ref[...],
            come_ref[...],
            step * group,
        )
        for tile, north in enumerate(values):
            at = step * group + tile
            south = south_ref[at]
            result[2 * at] = jnp.where(low, south, pltpu.roll(north, rows // 2, 0))
            result[2 * at + 1] = jnp.where(low, pltpu.roll(south, rows // 2, 0), north)
        copy_of(step).start()
        return carry

    lax.fori_loop(0, count, body, 0)
    for step in range(count):
        copy_of(step).wait()


def advect_north(first, offset, own, near, far, stay, come, south, whole):
    pairs, height, cols = own.shape
    count = 2 * pairs // stay.shape[0]
    return pl.pallas_call(
        functools.partial(advect_north_kernel, first),
        out_shape=jax.ShapeDtypeStruct(whole.shape, F32),
        in_specs=[pl.BlockSpec(memory_space=pltpu.SMEM)] + [vmem()] * 6 + [any_space()],
        out_specs=any_space(),
        scratch_shapes=[
            pltpu.VMEM((4 * pairs, height // 2, cols), F32),
            pltpu.SemaphoreType.DMA((count,)),
        ],
        input_output_aliases={7: 0},
        compiler_params=params(16),
        cost_estimate=cost(1 << 22, 4 << 20),
    )(offset, own, near, far, stay, come, south, whole)


def shifted(value, axis, steps):
    count = lax.axis_size(axis)
    return lax.ppermute(value, axis, [(i, (i + steps) % count) for i in range(count)])


def passed_along(block, axis, distance):
    devices = range(lax.axis_size(axis))
    return lax.ppermute(
        block, axis, [(i, i + distance) for i in devices if i + distance in devices]
    )


def on_device(
    state,
    surface,
    layer_one,
    layer_two,
    layer_three,
    layer_four,
    layer_five,
    lit_columns,
    row_offset,
):
    return tile_step(
        state,
        surface,
        (layer_one, layer_two, layer_three, layer_four),
        layer_five,
        lit_columns,
        row_offset,
    )


def tile_step(state, surface, layers, layer_five, lit_columns, row_offset):
    fields, levels, rows, cols = state.shape
    slots = lit_columns.reshape(1, rows * cols)
    flat = state.reshape(fields * levels, rows, cols)

    start_winds = state[:3]
    to_south, to_north, to_west, to_east = messages(start_winds)
    rest, lit, ozone = rest_features(state, surface, slots)
    from_east = shifted(to_west, "lon", -1)
    from_west = shifted(to_east, "lon", 1)
    from_south = shifted(to_north, "lat", 1)
    from_north = passed_along(to_south, "lat", -1)
    ozone_near = shifted(ozone, "lon", 1)
    strips, strips_south, strips_north = strips_of(to_west, to_east, from_east, from_west)
    strips_from_south = shifted(strips_north, "lat", 1)
    strips_from_north = passed_along(strips_south, "lat", -1)

    five = layer_five.T
    five_tracers = five[2 * levels : 6 * levels]
    five_winds = jnp.concatenate([five[: 2 * levels], five[6 * levels :]], axis=0)

    inner_out = inner(start_winds, from_north, from_south)
    ozone_relay = relay(row_offset, ozone, ozone_near, 0, rows)
    ozone_far = shifted(ozone_relay, "lon", 2)
    winds, upwind, features, hidden_south, first = network(
        inner_out,
        (strips, strips_from_north, strips_from_south),
        rest,
        layers,
        five_tracers,
        lit,
        flat,
    )
    first_near = shifted(first, "lon", 1)
    hidden_north, other = second(3 * levels, features, layers, five_tracers, lit, flat)
    other_near = shifted(other, "lon", 1)
    first_relay = relay(row_offset, first, first_near, 0, rows // 2)
    first_far = shifted(first_relay, "lon", 2)
    other_relay = relay(row_offset, other, other_near, rows // 2, rows // 2)
    other_far = shifted(other_relay, "lon", 2)
    whole, flux, stay, come, stay_south, come_south, stay_north, come_north = winds_out(
        hidden_south, hidden_north, five_winds, lit, winds, upwind, fields
    )
    whole = advect_ozone(fields - 1, row_offset, ozone, ozone_near, ozone_far, stay, come, whole)
    south = advect_south(row_offset, first, first_near, first_far, stay_south, come_south)
    whole = advect_north(
        3, row_offset, other, other_near, other_far, stay_north, come_north, south, whole
    )
    return whole.reshape(fields, levels, rows, cols), flux


def solution(mesh):
    in_specs = (
        P(None, None, "lat", "lon"),
        P(None, "lat", "lon"),
        P(),
        P(),
        P(),
        P(),
        P(),
        P("lat", "lon", None),
        P("lat"),
    )
    out_specs = (P(None, None, "lat", "lon"), P(None, "lat", "lon"))
    return jax.shard_map(
        on_device, mesh=mesh, in_specs=in_specs, out_specs=out_specs, check_vma=False
    )
```

```python
import functools

import jax
import jax.numpy as jnp
from jax import lax
from jax.experimental import pallas as pl
from jax.experimental.pallas import tpu as pltpu
from jax.sharding import PartitionSpec as P


SUBSTEPS = 4
SOUND_COURANT = 0.6
PHYSICS_STEP = 0.5
LEAK_SLOPE = 0.15

STRIP = 6 * SUBSTEPS
F32 = jnp.float32
BF16 = jnp.bfloat16


def vmem():
    return pl.BlockSpec(memory_space=pltpu.VMEM)


def any_space():
    return pl.BlockSpec(memory_space=pl.ANY)


def params(mib):
    return pltpu.CompilerParams(vmem_limit_bytes=mib << 20)


def cost(flops, nbytes):
    return pl.CostEstimate(flops=flops, bytes_accessed=nbytes, transcendentals=0)


def iota(shape, dim):
    return lax.broadcasted_iota(jnp.int32, shape, dim)


def back(shift, size):
    return (size - shift) % size


def paired(tiles, rows, low):
    tiles = tiles.reshape((tiles.shape[0] // 2, 2) + tiles.shape[1:])
    even = tiles[:, 0]
    odd = pltpu.roll(tiles[:, 1], rows // 2, 1)
    return jnp.where(low, even, odd), jnp.where(low, odd, even)


def halo_rows(north_pair, south_pair, low):
    even = jnp.where(low, north_pair, south_pair)
    odd = pltpu.roll(jnp.where(low, south_pair, north_pair), north_pair.shape[-2] // 2, 1)
    return jnp.stack([even, odd], axis=1).reshape((-1,) + even.shape[1:])


def side_packs(tiles, lane):
    per = tiles.shape[-1] // STRIP
    west_packs, east_packs = [], []
    for pack in range(tiles.shape[0] // per):
        west = jnp.zeros(tiles.shape[1:], F32)
        east = jnp.zeros(tiles.shape[1:], F32)
        for slot in range(per):
            tile = tiles[pack * per + slot]
            start = slot * STRIP
            inside = (lane >= start) & (lane < start + STRIP)
            west = jnp.where(inside, pltpu.roll(tile, start + 2 * SUBSTEPS, 1), west)
            east = jnp.where(inside, pltpu.roll(tile, start + 4 * SUBSTEPS, 1), east)
        west_packs.append(west)
        east_packs.append(east)
    return jnp.stack(west_packs), jnp.stack(east_packs)


def tall(tiles):
    count, rows, cols = tiles.shape
    return tiles.reshape(count // 2, 2 * rows, cols).astype(BF16)


def messages_kernel(winds_ref, south_ref, north_ref, west_ref, east_ref):
    fields, levels, rows, cols = winds_ref.shape
    low = iota((rows, cols), 0) < rows // 2
    lane = iota((rows, cols), 1)
    held = winds_ref.reshape(fields * levels, rows, cols)

    def body(step, carry):
        tiles = held[pl.ds(step * 20, 20)]
        south, north = paired(tiles, rows, low)
        south_ref[pl.ds(step * 5, 5)] = tall(south)
        north_ref[pl.ds(step * 5, 5)] = tall(north)
        west, east = side_packs(tiles, lane)
        west_ref[pl.ds(step * 2, 2)] = tall(west)
        east_ref[pl.ds(step * 2, 2)] = tall(east)
        return carry

    steps = fields * levels // 20
    lax.fori_loop(0, steps, body, 0, unroll=steps)


def messages(winds):
    fields, levels, rows, cols = winds.shape

    def shape(count):
        return jax.ShapeDtypeStruct((count // 2, 2 * rows, cols), BF16)

    packs = fields * levels // (cols // STRIP)
    return pl.pallas_call(
        messages_kernel,
        out_shape=(shape(fields * levels // 2),) * 2 + (shape(packs),) * 2,
        in_specs=[vmem()],
        out_specs=(vmem(),) * 4,
        compiler_params=params(4),
        cost_estimate=cost(1 << 20, 2 << 20),
    )(winds)


def short(ref, at, size):
    rows, cols = ref.shape[1] // 2, ref.shape[2]
    return ref[pl.ds(at // 2, size // 2)].astype(F32).reshape(size, rows, cols)


def strips_kernel(own_west_ref, own_east_ref, from_east_ref, from_west_ref, out_ref, south_ref, north_ref):
    count = 2 * own_west_ref.shape[0]
    rows, cols = own_west_ref.shape[1] // 2, own_west_ref.shape[2]
    place = iota((rows, cols), 1) % STRIP
    low = iota((rows, cols), 0) < rows // 2
    value = short(own_east_ref, 0, count)
    value = jnp.where(place < 4 * SUBSTEPS, short(from_west_ref, 0, count), value)
    value = jnp.where(place < 3 * SUBSTEPS, short(from_east_ref, 0, count), value)
    value = jnp.where(place < 2 * SUBSTEPS, short(own_west_ref, 0, count), value)
    out_ref[...] = value
    south, north = paired(value, rows, low)
    south_ref[...] = tall(south)
    north_ref[...] = tall(north)


def strips_of(own_west, own_east, from_east, from_west):
    count, height, cols = own_west.shape
    half = jax.ShapeDtypeStruct((count // 2, height, cols), BF16)
    return pl.pallas_call(
        strips_kernel,
        out_shape=(jax.ShapeDtypeStruct((2 * count, height // 2, cols), F32), half, half),
        in_specs=[vmem()] * 4,
        out_specs=(vmem(),) * 3,
        compiler_params=params(4),
        cost_estimate=cost(1 << 20, 1 << 20),
    )(own_west, own_east, from_east, from_west)


def open_rows(rows, cols):
    place = iota((2 * rows, cols), 0)
    offset = jnp.where(place < rows + rows // 2, place, place - 2 * rows)
    row = lax.axis_index("lat") * rows + offset
    last = rows * lax.axis_size("lat") - 1
    return jnp.where((row >= 0) & (row < last), 1.0, 0.0).astype(F32)


def substeps(zonal, merid, press, free):
    rows, cols = zonal.shape[-2:]
    for _ in range(SUBSTEPS):
        zonal = zonal - SOUND_COURANT * (pltpu.roll(press, cols - 1, 2) - press)
        merid = (merid - SOUND_COURANT * (pltpu.roll(press, rows - 1, 1) - press)) * free
        press = press - SOUND_COURANT * (
            zonal - pltpu.roll(zonal, 1, 2) + merid - pltpu.roll(merid, 1, 1)
        )
    return zonal, merid, press


def inner_kernel(state_ref, from_north_ref, from_south_ref, out_ref):
    levels = state_ref.shape[1]
    rows, cols = state_ref.shape[2:]
    low = iota((rows, cols), 0) < rows // 2
    free = open_rows(rows, cols)
    parts = []
    for field in range(3):
        at = pl.ds(field * (levels // 4), levels // 4)
        north = from_north_ref[at].astype(F32).reshape(levels // 2, rows, cols)
        south = from_south_ref[at].astype(F32).reshape(levels // 2, rows, cols)
        side = halo_rows(north, south, low)
        parts.append(jnp.concatenate([state_ref[field], side], axis=1))
    for field, value in enumerate(substeps(*parts, free)):
        out_ref[field] = value[:, :rows]


def inner(state, from_north, from_south):
    _, levels, rows, cols = state.shape
    return pl.pallas_call(
        inner_kernel,
        out_shape=jax.ShapeDtypeStruct((3, levels, rows, cols), F32),
        in_specs=[vmem()] * 3,
        out_specs=vmem(),
        compiler_params=params(16),
        cost_estimate=cost(1 << 24, 4 << 20),
    )(state, from_north, from_south)


def rest_kernel(state_ref, surface_ref, slots_ref, rest_ref, lit_ref, ozone_ref, buffer, wide):
    fields, levels, rows, cols = state_ref.shape
    ozone_ref[...] = tall(state_ref[fields - 1])
    extra = surface_ref.shape[0]
    first = 3 * levels
    wide[...] = surface_ref[...].astype(F32).reshape(extra * rows, cols)
    flat = state_ref.reshape(fields * levels * rows, cols)
    buffer[0:first] = jnp.zeros((first, cols), F32)
    for row in range(rows):
        buffer[first : fields * levels] = flat[
            pl.ds(first * rows + row, (fields - 3) * levels, stride=rows), :
        ]
        buffer[fields * levels : fields * levels + extra] = wide[pl.ds(row, extra, stride=rows), :]
        rest_ref[:, row * cols : (row + 1) * cols] = buffer[...].astype(BF16)
    slots = slots_ref[...]
    count = slots.shape[1]
    in_row = (slots // cols == iota((rows, count), 0)).astype(F32).astype(BF16)
    in_col = (slots % cols == iota((cols, count), 0)).astype(F32).astype(BF16)
    lit_ref[...] = lax.dot_general(
        in_row, in_col, (((1,), (1,)), ((), ())), preferred_element_type=F32
    )


def rest_features(state, surface, slots):
    fields, levels, rows, cols = state.shape
    count = fields * levels + surface.shape[0]
    return pl.pallas_call(
        rest_kernel,
        out_shape=(
            jax.ShapeDtypeStruct((count, rows * cols), BF16),
            jax.ShapeDtypeStruct((rows, cols), F32),
            jax.ShapeDtypeStruct((levels // 2, 2 * rows, cols), BF16),
        ),
        in_specs=[vmem()] * 3,
        out_specs=(vmem(),) * 3,
        scratch_shapes=[
            pltpu.VMEM((count, cols), F32),
            pltpu.VMEM((surface.shape[0] * rows, cols), F32),
        ],
        compiler_params=params(12),
        cost_estimate=cost(1 << 24, 4 << 20),
    )(state, surface, slots)


def leaky(value):
    return jnp.maximum(value, LEAK_SLOPE * value).astype(BF16)


def half_tiles(tiles, low, north):
    rows = tiles.shape[1]
    tiles = tiles.reshape((tiles.shape[0] // 2, 2) + tiles.shape[1:])
    even, odd = tiles[:, 0], tiles[:, 1]
    if north:
        return jnp.where(low, pltpu.roll(even, rows // 2, 1), odd)
    return jnp.where(low, even, pltpu.roll(odd, rows // 2, 1))


def half_step(features_ref, layers, five_ref, lit_ref, state_ref, first, north, hidden_ref, tracer_ref, spread):
    rows, cols = lit_ref.shape
    half = rows // 2
    levels = five_ref.shape[0]
    low = iota((rows, cols), 0) < half
    at = half * cols if north else 0
    hidden = leaky(
        lax.dot_general(
            features_ref[:, at : at + half * cols],
            layers[0][...],
            (((0,), (0,)), ((), ())),
            preferred_element_type=F32,
        )
    )
    for weight in layers[1:]:
        hidden = leaky(jnp.dot(hidden, weight[...], preferred_element_type=F32))
    hidden_ref[...] = hidden
    result = lax.dot_general(
        five_ref[...], hidden, (((1,), (1,)), ((), ())), preferred_element_type=F32
    )
    for row in range(half):
        spread[pl.ds(row, levels, stride=half), :] = result[:, row * cols : (row + 1) * cols]
    lit = lit_ref[...]
    other = pltpu.roll(lit, half, 0)
    lit = jnp.where(low, other, lit) if north else jnp.where(low, lit, other)

    def body(step, carry):
        value = spread[pl.ds(step * 10 * rows, 10 * rows), :].reshape(10, rows, cols)
        value = jnp.where(lit > 0.5, value.astype(BF16).astype(F32), 0.0)
        held = half_tiles(state_ref[pl.ds(first + step * 20, 20)], low, north)
        tracer_ref[pl.ds(step * 5, 5)] = tall(held + PHYSICS_STEP * value)
        return carry

    lax.fori_loop(0, levels // 20, body, 0, unroll=3)


def network_kernel(
    inner_ref,
    here_ref,
    north_ref,
    south_ref,
    rest_ref,
    one_ref,
    two_ref,
    three_ref,
    four_ref,
    five_ref,
    lit_ref,
    state_ref,
    winds_ref,
    upwind_ref,
    features,
    hidden_ref,
    tracer_ref,
    strips,
    spread,
):
    _, levels, rows, cols = inner_ref.shape
    per = cols // STRIP
    packs = levels // per
    low = iota((rows, cols), 0) < rows // 2
    free = open_rows(rows, cols)
    parts = []
    for field in range(3):
        half = [short(ref, field * packs // 2, packs // 2) for ref in (north_ref, south_ref)]
        here = here_ref[pl.ds(field * packs, packs)]
        parts.append(jnp.concatenate([here, halo_rows(*half, low)], axis=1))
    for field, value in enumerate(substeps(*parts, free)):
        strips[field] = value[:, :rows]
    lane = iota((rows, cols), 1)

    def merge(step, carry):
        for slot in range(per):
            level = step * per + slot
            for field in range(3):
                strip = strips[field, step]
                west = pltpu.roll(strip, back(slot * STRIP + 4 * SUBSTEPS, cols), 1)
                east = pltpu.roll(strip, back(slot * STRIP + 2 * SUBSTEPS, cols), 1)
                value = inner_ref[field, level]
                value = jnp.where(lane < SUBSTEPS, west, value)
                value = jnp.where(lane >= cols - SUBSTEPS, east, value)
                winds_ref[pl.ds((field * levels + level) * rows, rows), :] = value
                if field == 0:
                    upwind_ref[level] = pltpu.roll(jnp.where(lane == cols - 1, west, value), 1, 1)
        return carry

    lax.fori_loop(0, packs, merge, 0, unroll=packs)
    count = 3 * levels
    features[...] = rest_ref[...]
    for row in range(rows):
        features[0:count, row * cols : (row + 1) * cols] = winds_ref[
            pl.ds(row, count, stride=rows), :
        ].astype(BF16)
    half_step(
        features,
        (one_ref, two_ref, three_ref, four_ref),
        five_ref,
        lit_ref,
        state_ref,
        3 * levels,
        False,
        hidden_ref,
        tracer_ref,
        spread,
    )


def network(inner_out, strips, rest, layers, five, lit, flat):
    _, levels, rows, cols = inner_out.shape
    count = five.shape[0]
    return pl.pallas_call(
        network_kernel,
        out_shape=(
            jax.ShapeDtypeStruct((3 * levels * rows, cols), F32),
            jax.ShapeDtypeStruct((levels, rows, cols), F32),
            jax.ShapeDtypeStruct(rest.shape, BF16),
            jax.ShapeDtypeStruct((rows * cols // 2, layers[3].shape[1]), BF16),
            jax.ShapeDtypeStruct((count // 4, 2 * rows, cols), BF16),
        ),
        in_specs=[vmem()] * 12,
        out_specs=(vmem(),) * 5,
        scratch_shapes=[
            pltpu.VMEM((3, levels * STRIP // (cols - cols % STRIP), rows, cols), F32),
            pltpu.VMEM((count * rows // 2, cols), F32),
        ],
        compiler_params=params(32),
        cost_estimate=cost(3 << 30, 8 << 20),
    )(inner_out, *strips, rest, *layers, five, lit, flat)


def second_kernel(
    first, features_ref, one_ref, two_ref, three_ref, four_ref, five_ref, lit_ref, state_ref,
    hidden_ref, tracer_ref, spread,
):
    layers = (one_ref, two_ref, three_ref, four_ref)
    half_step(
        features_ref, layers, five_ref, lit_ref, state_ref, first, True, hidden_ref, tracer_ref, spread
    )


def second(first, features, layers, five, lit, flat):
    rows, cols = lit.shape
    count = five.shape[0]
    return pl.pallas_call(
        functools.partial(second_kernel, first),
        out_shape=(
            jax.ShapeDtypeStruct((rows * cols // 2, layers[3].shape[1]), BF16),
            jax.ShapeDtypeStruct((count // 4, 2 * rows, cols), BF16),
        ),
        in_specs=[vmem()] * 8,
        out_specs=(vmem(),) * 2,
        scratch_shapes=[pltpu.VMEM((count * rows // 2, cols), F32)],
        compiler_params=params(24),
        cost_estimate=cost(2 << 30, 6 << 20),
    )(features, *layers, five, lit, flat)


def winds_kernel(
    south_ref, north_ref, five_ref, lit_ref, winds_ref, upwind_ref, out_ref, flux_ref,
    stay_ref, come_ref, stay_south_ref, come_south_ref, stay_north_ref, come_north_ref,
    spread, updated, sem
):
    rows, cols = lit_ref.shape
    levels = upwind_ref.shape[0]
    fluxes = flux_ref.shape[0]
    count = five_ref.shape[0]
    for side, hidden_ref in enumerate((south_ref, north_ref)):
        result = lax.dot_general(
            five_ref[...], hidden_ref[...], (((1,), (1,)), ((), ())), preferred_element_type=F32
        )
        for row in range(rows // 2):
            spread[pl.ds(side * (rows // 2) + row, count, stride=rows), :] = result[
                :, row * cols : (row + 1) * cols
            ]
    lit = lit_ref[...] > 0.5
    low = iota((rows, cols), 0) < rows // 2

    def body(step, carry):
        value = spread[pl.ds(step * 10 * rows, 10 * rows), :].reshape(10, rows, cols)
        value = jnp.where(lit, value.astype(BF16).astype(F32), 0.0)
        wind = winds_ref[pl.ds(step * 10 * rows, 10 * rows), :].reshape(10, rows, cols)
        updated[pl.ds(step * 10, 10)] = wind + PHYSICS_STEP * value
        return carry

    lax.fori_loop(0, 2 * levels // 10, body, 0)
    updated[2 * levels : 3 * levels] = winds_ref[2 * levels * rows :, :].reshape(
        levels, rows, cols
    )
    copy = pltpu.make_async_copy(
        updated, out_ref.at[pl.ds(0, 3 * levels)], sem
    )
    copy.start()
    value = spread[2 * levels * rows :, :].reshape(fluxes, rows, cols)
    flux_ref[...] = jnp.where(lit, value, 0.0).astype(BF16)

    def share(step, carry):
        here = winds_ref[pl.ds(step * 10 * rows, 10 * rows), :].reshape(10, rows, cols)
        stay = 0.5 - 0.45 * jnp.tanh(here)
        come = 0.5 + 0.45 * jnp.tanh(upwind_ref[pl.ds(step * 10, 10)])
        stay_ref[pl.ds(step * 10, 10)] = stay
        come_ref[pl.ds(step * 10, 10)] = come
        stay_south_ref[pl.ds(step * 5, 5)] = half_tiles(stay, low, False)
        come_south_ref[pl.ds(step * 5, 5)] = half_tiles(come, low, False)
        stay_north_ref[pl.ds(step * 5, 5)] = half_tiles(stay, low, True)
        come_north_ref[pl.ds(step * 5, 5)] = half_tiles(come, low, True)
        return carry

    lax.fori_loop(0, levels // 10, share, 0)
    copy.wait()


def winds_out(hidden_south, hidden_north, five, lit, winds, upwind, fields):
    levels, rows, cols = upwind.shape
    fluxes = five.shape[0] - 2 * levels
    share = jax.ShapeDtypeStruct((levels, rows, cols), F32)
    part = jax.ShapeDtypeStruct((levels // 2, rows, cols), F32)
    return pl.pallas_call(
        winds_kernel,
        out_shape=(
            jax.ShapeDtypeStruct((fields * levels, rows, cols), F32),
            jax.ShapeDtypeStruct((fluxes, rows, cols), BF16),
            share,
            share,
            part,
            part,
            part,
            part,
        ),
        in_specs=[vmem()] * 6,
        out_specs=(any_space(),) + (vmem(),) * 7,
        scratch_shapes=[
            pltpu.VMEM((five.shape[0] * rows, cols), F32),
            pltpu.VMEM((3 * levels, rows, cols), F32),
            pltpu.SemaphoreType.DMA,
        ],
        compiler_params=params(16),
        cost_estimate=cost(1 << 28, 4 << 20),
    )(hidden_south, hidden_north, five, lit, winds, upwind)


def spread_offsets(offset_ref, shape, base, span):
    rows, cols = shape
    place = iota((rows, cols), 0) % span
    offset = jnp.zeros((rows, cols), jnp.int32)
    for row in range(span):
        offset = jnp.where(place == row, offset_ref[base + row], offset)
    return offset // cols, offset % cols


def along(value, index):
    return jnp.take_along_axis(value, index, axis=1, mode="promise_in_bounds")


def relay_kernel(base, span, offset_ref, own_ref, near_ref, out_ref):
    rows = own_ref.shape[1] // 2
    cols = own_ref.shape[2]
    pairs = own_ref.shape[0]
    blocks, cells = spread_offsets(offset_ref, (rows, cols), base, span)
    lane = iota((rows, cols), 1)
    take_near = (blocks >= 2) & (lane > cols - 1 - cells)
    edge = cols - 1 - cells

    def body(step, column):
        at = pl.ds(step * 10, 10)
        own = own_ref[at].astype(F32).reshape(20, rows, cols)
        near = near_ref[at].astype(F32).reshape(20, rows, cols)
        out_ref[at] = tall(jnp.where(take_near, near, own))
        for level in range(20):
            column = jnp.where(lane == step * 20 + level, along(near[level], edge), column)
        return column

    steps = pairs // 10
    column = lax.fori_loop(0, steps, body, jnp.zeros((rows, cols), F32), unroll=3)
    out_ref[pairs] = jnp.concatenate([column, column], axis=0).astype(BF16)


def relay(offset, own, near, base, span):
    pairs, height, cols = own.shape
    return pl.pallas_call(
        functools.partial(relay_kernel, base, span),
        out_shape=jax.ShapeDtypeStruct((pairs + 1, height, cols), BF16),
        in_specs=[pl.BlockSpec(memory_space=pltpu.SMEM), vmem(), vmem()],
        out_specs=vmem(),
        compiler_params=params(8),
        cost_estimate=cost(1 << 20, 1 << 20),
    )(offset, own, near)


def blend(offset_ref, shape, base, span):
    rows, cols = shape
    blocks, cells = spread_offsets(offset_ref, shape, base, span)
    lane = iota((rows, cols), 1)
    from_right = lane <= cols - 1 - cells
    index = (lane - cells) & (cols - 1)
    edge_index = cols - 1 - cells
    is_zero, is_one, is_two = blocks == 0, blocks == 1, blocks >= 2

    def tiles(own, near, far, column, stay, come, first):
        right = jnp.where(is_zero, own, jnp.where(is_one, near, far))
        left = jnp.where(is_zero, near, far)
        merged = jnp.where(from_right, right, left)
        edges = jnp.where(is_two, column, left)
        values = []
        for tile in range(own.shape[0]):
            which = jnp.where(is_two, first + tile, edge_index)
            here = along(merged[tile], index)
            behind = jnp.where(lane == 0, along(edges[tile], which), pltpu.roll(here, 1, 1))
            values.append(stay[tile] * here + come[tile] * behind)
        return values

    return tiles


def read_tiles(refs, step, group, shape):
    at = pl.ds(step * (group // 2), group // 2)
    return [ref[at].astype(F32).reshape((group,) + shape) for ref in refs]


def last_column(far_ref, pairs, rows):
    return far_ref[pairs].astype(F32)[:rows]


def advect_ozone_kernel(
    first, offset_ref, own_ref, near_ref, far_ref, stay_ref, come_ref, whole_ref, out_ref, result, sem
):
    levels, rows, cols = stay_ref.shape
    group = levels // 2
    tiles = blend(offset_ref, (rows, cols), 0, rows)
    column = last_column(far_ref, own_ref.shape[0], rows)
    copies = []
    for step in range(2):
        share = pl.ds(step * group, group)
        values = tiles(
            *read_tiles((own_ref, near_ref, far_ref), step, group, (rows, cols)),
            column,
            stay_ref[share],
            come_ref[share],
            step * group,
        )
        for tile, value in enumerate(values):
            result[step * group + tile] = value
        copy = pltpu.make_async_copy(
            result.at[share], out_ref.at[pl.ds(first * levels + step * group, group)], sem.at[step]
        )
        copy.start()
        copies.append(copy)
    for copy in copies:
        copy.wait()


def advect_ozone(first, offset, own, near, far, stay, come, whole):
    levels, rows, cols = stay.shape
    return pl.pallas_call(
        functools.partial(advect_ozone_kernel, first),
        out_shape=jax.ShapeDtypeStruct(whole.shape, F32),
        in_specs=[pl.BlockSpec(memory_space=pltpu.SMEM)] + [vmem()] * 5 + [any_space()],
        out_specs=any_space(),
        scratch_shapes=[pltpu.VMEM((levels, rows, cols), F32), pltpu.SemaphoreType.DMA((2,))],
        input_output_aliases={6: 0},
        compiler_params=params(8),
        cost_estimate=cost(1 << 22, 2 << 20),
    )(offset, own, near, far, stay, come, whole)


def advect_south_kernel(offset_ref, own_ref, near_ref, far_ref, stay_ref, come_ref, out_ref):
    group, rows, cols = stay_ref.shape
    pairs = own_ref.shape[0]
    tiles = blend(offset_ref, (rows, cols), 0, rows // 2)
    column = last_column(far_ref, pairs, rows)

    def body(step, carry):
        values = tiles(
            *read_tiles((own_ref, near_ref, far_ref), step, group, (rows, cols)),
            column,
            stay_ref[...],
            come_ref[...],
            step * group,
        )
        for tile, value in enumerate(values):
            out_ref[step * group + tile] = value
        return carry

    lax.fori_loop(0, 2 * pairs // group, body, 0)


def advect_south(offset, own, near, far, stay, come):
    pairs, height, cols = own.shape
    return pl.pallas_call(
        advect_south_kernel,
        out_shape=jax.ShapeDtypeStruct((2 * pairs, height // 2, cols), F32),
        in_specs=[pl.BlockSpec(memory_space=pltpu.SMEM)] + [vmem()] * 5,
        out_specs=vmem(),
        compiler_params=params(8),
        cost_estimate=cost(1 << 22, 2 << 20),
    )(offset, own, near, far, stay, come)


def advect_north_kernel(
    first, offset_ref, own_ref, near_ref, far_ref, stay_ref, come_ref, south_ref, whole_ref, out_ref,
    result, sem,
):
    group, rows, cols = stay_ref.shape
    pairs = own_ref.shape[0]
    tiles = blend(offset_ref, (rows, cols), rows // 2, rows // 2)
    column = last_column(far_ref, pairs, rows)
    low = iota((rows, cols), 0) < rows // 2
    count = 2 * pairs // group

    def copy_of(step):
        span = pl.ds(step * 2 * group, 2 * group)
        return pltpu.make_async_copy(
            result.at[span],
            out_ref.at[pl.ds((first + step) * 2 * group, 2 * group)],
            sem.at[step],
        )

    def body(step, carry):
        values = tiles(
            *read_tiles((own_ref, near_ref, far_ref), step, group, (rows, cols)),
            column,
            stay_ref[...],
            come_ref[...],
            step * group,
        )
        for tile, north in enumerate(values):
            at = step * group + tile
            south = south_ref[at]
            result[2 * at] = jnp.where(low, south, pltpu.roll(north, rows // 2, 0))
            result[2 * at + 1] = jnp.where(low, pltpu.roll(south, rows // 2, 0), north)
        copy_of(step).start()
        return carry

    lax.fori_loop(0, count, body, 0)
    for step in range(count):
        copy_of(step).wait()


def advect_north(first, offset, own, near, far, stay, come, south, whole):
    pairs, height, cols = own.shape
    count = 2 * pairs // stay.shape[0]
    return pl.pallas_call(
        functools.partial(advect_north_kernel, first),
        out_shape=jax.ShapeDtypeStruct(whole.shape, F32),
        in_specs=[pl.BlockSpec(memory_space=pltpu.SMEM)] + [vmem()] * 6 + [any_space()],
        out_specs=any_space(),
        scratch_shapes=[
            pltpu.VMEM((4 * pairs, height // 2, cols), F32),
            pltpu.SemaphoreType.DMA((count,)),
        ],
        input_output_aliases={7: 0},
        compiler_params=params(16),
        cost_estimate=cost(1 << 22, 4 << 20),
    )(offset, own, near, far, stay, come, south, whole)


def shifted(value, axis, steps):
    count = lax.axis_size(axis)
    return lax.ppermute(value, axis, [(i, (i + steps) % count) for i in range(count)])


def on_device(
    state,
    surface,
    layer_one,
    layer_two,
    layer_three,
    layer_four,
    layer_five,
    lit_columns,
    row_offset,
):
    return tile_step(
        state,
        surface,
        (layer_one, layer_two, layer_three, layer_four),
        layer_five,
        lit_columns,
        row_offset,
    )


def tile_step(state, surface, layers, layer_five, lit_columns, row_offset):
    fields, levels, rows, cols = state.shape
    slots = lit_columns.reshape(1, rows * cols)
    flat = state.reshape(fields * levels, rows, cols)

    start_winds = state[:3]
    to_south, to_north, to_west, to_east = messages(start_winds)
    rest, lit, ozone = rest_features(state, surface, slots)
    from_east = shifted(to_west, "lon", -1)
    from_west = shifted(to_east, "lon", 1)
    from_south = shifted(to_north, "lat", 1)
    from_north = shifted(to_south, "lat", -1)
    ozone_near = shifted(ozone, "lon", 1)
    strips, strips_south, strips_north = strips_of(to_west, to_east, from_east, from_west)
    strips_from_south = shifted(strips_north, "lat", 1)
    strips_from_north = shifted(strips_south, "lat", -1)

    five = layer_five.T
    five_tracers = five[2 * levels : 6 * levels]
    five_winds = jnp.concatenate([five[: 2 * levels], five[6 * levels :]], axis=0)

    inner_out = inner(start_winds, from_north, from_south)
    ozone_relay = relay(row_offset, ozone, ozone_near, 0, rows)
    ozone_far = shifted(ozone_relay, "lon", 2)
    winds, upwind, features, hidden_south, first = network(
        inner_out,
        (strips, strips_from_north, strips_from_south),
        rest,
        layers,
        five_tracers,
        lit,
        flat,
    )
    first_near = shifted(first, "lon", 1)
    hidden_north, other = second(3 * levels, features, layers, five_tracers, lit, flat)
    other_near = shifted(other, "lon", 1)
    first_relay = relay(row_offset, first, first_near, 0, rows // 2)
    first_far = shifted(first_relay, "lon", 2)
    other_relay = relay(row_offset, other, other_near, rows // 2, rows // 2)
    other_far = shifted(other_relay, "lon", 2)
    whole, flux, stay, come, stay_south, come_south, stay_north, come_north = winds_out(
        hidden_south, hidden_north, five_winds, lit, winds, upwind, fields
    )
    whole = advect_ozone(fields - 1, row_offset, ozone, ozone_near, ozone_far, stay, come, whole)
    south = advect_south(row_offset, first, first_near, first_far, stay_south, come_south)
    whole = advect_north(
        3, row_offset, other, other_near, other_far, stay_north, come_north, south, whole
    )
    return whole.reshape(fields, levels, rows, cols), flux


def solution(mesh):
    in_specs = (
        P(None, None, "lat", "lon"),
        P(None, "lat", "lon"),
        P(),
        P(),
        P(),
        P(),
        P(),
        P("lat", "lon", None),
        P("lat"),
    )
    out_specs = (P(None, None, "lat", "lon"), P(None, "lat", "lon"))
    return jax.shard_map(
        on_device, mesh=mesh, in_specs=in_specs, out_specs=out_specs, check_vma=False
    )
```

```python
import functools

import jax
import jax.numpy as jnp
from jax import lax
from jax.experimental import pallas as pl
from jax.experimental.pallas import tpu as pltpu
from jax.sharding import PartitionSpec as P


SUBSTEPS = 4
SOUND_COURANT = 0.6
PHYSICS_STEP = 0.5
LEAK_SLOPE = 0.15

STRIP = 6 * SUBSTEPS
F32 = jnp.float32
BF16 = jnp.bfloat16


def vmem():
    return pl.BlockSpec(memory_space=pltpu.VMEM)


def any_space():
    return pl.BlockSpec(memory_space=pl.ANY)


def params(mib):
    return pltpu.CompilerParams(vmem_limit_bytes=mib << 20)


def cost(flops, nbytes):
    return pl.CostEstimate(flops=flops, bytes_accessed=nbytes, transcendentals=0)


def iota(shape, dim):
    return lax.broadcasted_iota(jnp.int32, shape, dim)


def back(shift, size):
    return (size - shift) % size


def halo_messages(zonal, merid, press):
    rows, cols = zonal.shape[1:]
    place = iota((rows, cols), 0)
    above = pltpu.roll(merid, 1, 1)
    spread = zonal - pltpu.roll(zonal, 1, 2) + merid - jnp.where(place == 0, 0.0, above)
    turned = pltpu.roll(spread, rows // 2, 1)
    south = jnp.where(place < rows // 2, press, turned)
    north = jnp.where(place == 0, above, jnp.where(place < rows // 2, turned, press))
    return south, north


def side_packs(tiles, lane):
    per = tiles.shape[-1] // STRIP
    west_packs, east_packs = [], []
    for pack in range(tiles.shape[0] // per):
        west = jnp.zeros(tiles.shape[1:], F32)
        east = jnp.zeros(tiles.shape[1:], F32)
        for slot in range(per):
            tile = tiles[pack * per + slot]
            start = slot * STRIP
            inside = (lane >= start) & (lane < start + STRIP)
            west = jnp.where(inside, pltpu.roll(tile, start + 2 * SUBSTEPS, 1), west)
            east = jnp.where(inside, pltpu.roll(tile, start + 4 * SUBSTEPS, 1), east)
        west_packs.append(west)
        east_packs.append(east)
    return jnp.stack(west_packs), jnp.stack(east_packs)


def tall(tiles):
    count, rows, cols = tiles.shape
    return tiles.reshape(count // 2, 2 * rows, cols).astype(BF16)


def messages_kernel(winds_ref, south_ref, north_ref, west_ref, east_ref):
    fields, levels, rows, cols = winds_ref.shape
    lane = iota((rows, cols), 1)
    free = open_rows(rows, cols)[:rows]
    packs = levels // (cols // STRIP)
    for field in range(fields):
        west, east = side_packs(winds_ref[field], lane)
        at = pl.ds(field * packs // 2, packs // 2)
        west_ref[at] = tall(west)
        east_ref[at] = tall(east)
    south, north = halo_messages(winds_ref[0], winds_ref[1] * free, winds_ref[2])
    south_ref[...] = tall(south)
    north_ref[...] = tall(north)


def messages(winds):
    fields, levels, rows, cols = winds.shape

    def shape(count):
        return jax.ShapeDtypeStruct((count // 2, 2 * rows, cols), BF16)

    packs = fields * levels // (cols // STRIP)
    return pl.pallas_call(
        messages_kernel,
        out_shape=(shape(levels),) * 2 + (shape(packs),) * 2,
        in_specs=[vmem()],
        out_specs=(vmem(),) * 4,
        compiler_params=params(4),
        cost_estimate=cost(1 << 20, 2 << 20),
    )(winds)


def short(ref, at, size):
    rows, cols = ref.shape[1] // 2, ref.shape[2]
    return ref[pl.ds(at // 2, size // 2)].astype(F32).reshape(size, rows, cols)


def strips_kernel(own_west_ref, own_east_ref, from_east_ref, from_west_ref, out_ref, south_ref, north_ref):
    count = 2 * own_west_ref.shape[0]
    rows, cols = own_west_ref.shape[1] // 2, own_west_ref.shape[2]
    place = iota((rows, cols), 1) % STRIP
    value = short(own_east_ref, 0, count)
    value = jnp.where(place < 4 * SUBSTEPS, short(from_west_ref, 0, count), value)
    value = jnp.where(place < 3 * SUBSTEPS, short(from_east_ref, 0, count), value)
    value = jnp.where(place < 2 * SUBSTEPS, short(own_west_ref, 0, count), value)
    out_ref[...] = value
    free = open_rows(rows, cols)[:rows]
    packs = count // 3
    south, north = halo_messages(value[:packs], value[packs : 2 * packs] * free, value[2 * packs :])
    south_ref[...] = tall(south)
    north_ref[...] = tall(north)


def strips_of(own_west, own_east, from_east, from_west):
    count, height, cols = own_west.shape
    half = jax.ShapeDtypeStruct((count // 3, height, cols), BF16)
    return pl.pallas_call(
        strips_kernel,
        out_shape=(jax.ShapeDtypeStruct((2 * count, height // 2, cols), F32), half, half),
        in_specs=[vmem()] * 4,
        out_specs=(vmem(),) * 3,
        compiler_params=params(4),
        cost_estimate=cost(1 << 20, 1 << 20),
    )(own_west, own_east, from_east, from_west)


def open_rows(rows, cols):
    place = iota((2 * rows, cols), 0)
    offset = jnp.where(place < rows + rows // 2, place, place - 2 * rows)
    row = lax.axis_index("lat") * rows + offset
    last = rows * lax.axis_size("lat") - 1
    return jnp.where((row >= 0) & (row < last), 1.0, 0.0).astype(F32)


def substeps(zonal, merid, press, from_north, from_south, free):
    rows, cols = zonal.shape[1:]
    place = iota((rows, cols), 0)
    low = place < rows // 2
    merid = merid * free[:rows]
    above = pltpu.roll(merid, 1, 1)
    south_free = pltpu.roll(free[rows:], 1, 0)
    spread = zonal - pltpu.roll(zonal, 1, 2) + merid
    spread = spread - jnp.where(place == 0, from_south * south_free, above)
    side = pltpu.roll(jnp.where(low, from_south, from_north), rows // 2, 1)
    side = jnp.where(place == 0, side - above, side)
    spread = jnp.concatenate([spread, side], axis=1)
    press = jnp.concatenate([press, jnp.where(low, from_north, from_south)], axis=1)
    total = None
    for _ in range(SUBSTEPS):
        total = press if total is None else total + press
        east = pltpu.roll(press, cols - 1, 2) - press
        north = (pltpu.roll(press, 2 * rows - 1, 1) - press) * free
        bend = east - pltpu.roll(east, 1, 2) + north - pltpu.roll(north, 1, 1)
        spread = spread - SOUND_COURANT * bend
        press = press - SOUND_COURANT * spread
    east = pltpu.roll(total, cols - 1, 2) - total
    north = (pltpu.roll(total, 2 * rows - 1, 1) - total) * free
    zonal = zonal - SOUND_COURANT * east[:, :rows]
    merid = merid - SOUND_COURANT * north[:, :rows]
    return zonal, merid, press[:, :rows]


def inner_kernel(state_ref, from_north_ref, from_south_ref, out_ref):
    levels = state_ref.shape[1]
    rows, cols = state_ref.shape[2:]
    parts = [state_ref[field] for field in range(3)]
    parts += [short(ref, 0, levels) for ref in (from_north_ref, from_south_ref)]
    for field, value in enumerate(substeps(*parts, open_rows(rows, cols))):
        out_ref[field] = value


def inner(state, from_north, from_south):
    _, levels, rows, cols = state.shape
    return pl.pallas_call(
        inner_kernel,
        out_shape=jax.ShapeDtypeStruct((3, levels, rows, cols), F32),
        in_specs=[vmem()] * 3,
        out_specs=vmem(),
        compiler_params=params(16),
        cost_estimate=cost(1 << 24, 4 << 20),
    )(state, from_north, from_south)


def rest_kernel(state_ref, surface_ref, slots_ref, rest_ref, lit_ref, ozone_ref, buffer, wide):
    fields, levels, rows, cols = state_ref.shape
    ozone_ref[...] = tall(state_ref[fields - 1])
    extra = surface_ref.shape[0]
    first = 3 * levels
    wide[...] = surface_ref[...].astype(F32).reshape(extra * rows, cols)
    flat = state_ref.reshape(fields * levels * rows, cols)
    buffer[0:first] = jnp.zeros((first, cols), F32)
    for row in range(rows):
        buffer[first : fields * levels] = flat[
            pl.ds(first * rows + row, (fields - 3) * levels, stride=rows), :
        ]
        buffer[fields * levels : fields * levels + extra] = wide[pl.ds(row, extra, stride=rows), :]
        rest_ref[:, row * cols : (row + 1) * cols] = buffer[...].astype(BF16)
    slots = slots_ref[...]
    count = slots.shape[1]
    in_row = (slots // cols == iota((rows, count), 0)).astype(F32).astype(BF16)
    in_col = (slots % cols == iota((cols, count), 0)).astype(F32).astype(BF16)
    lit_ref[...] = lax.dot_general(
        in_row, in_col, (((1,), (1,)), ((), ())), preferred_element_type=F32
    )


def rest_features(state, surface, slots):
    fields, levels, rows, cols = state.shape
    count = fields * levels + surface.shape[0]
    return pl.pallas_call(
        rest_kernel,
        out_shape=(
            jax.ShapeDtypeStruct((count, rows * cols), BF16),
            jax.ShapeDtypeStruct((rows, cols), F32),
            jax.ShapeDtypeStruct((levels // 2, 2 * rows, cols), BF16),
        ),
        in_specs=[vmem()] * 3,
        out_specs=(vmem(),) * 3,
        scratch_shapes=[
            pltpu.VMEM((count, cols), F32),
            pltpu.VMEM((surface.shape[0] * rows, cols), F32),
        ],
        compiler_params=params(12),
        cost_estimate=cost(1 << 24, 4 << 20),
    )(state, surface, slots)


def leaky(value):
    return jnp.maximum(value, LEAK_SLOPE * value).astype(BF16)


def half_tiles(tiles, low, north):
    rows = tiles.shape[1]
    tiles = tiles.reshape((tiles.shape[0] // 2, 2) + tiles.shape[1:])
    even, odd = tiles[:, 0], tiles[:, 1]
    if north:
        return jnp.where(low, pltpu.roll(even, rows // 2, 1), odd)
    return jnp.where(low, even, pltpu.roll(odd, rows // 2, 1))


def half_step(features_ref, layers, five_ref, lit_ref, state_ref, first, north, hidden_ref, tracer_ref, spread):
    rows, cols = lit_ref.shape
    half = rows // 2
    levels = five_ref.shape[0]
    low = iota((rows, cols), 0) < half
    at = half * cols if north else 0
    hidden = leaky(
        lax.dot_general(
            features_ref[:, at : at + half * cols],
            layers[0][...],
            (((0,), (0,)), ((), ())),
            preferred_element_type=F32,
        )
    )
    for weight in layers[1:]:
        hidden = leaky(jnp.dot(hidden, weight[...], preferred_element_type=F32))
    hidden_ref[...] = hidden
    result = lax.dot_general(
        five_ref[...], hidden, (((1,), (1,)), ((), ())), preferred_element_type=F32
    )
    for row in range(half):
        spread[pl.ds(row, levels, stride=half), :] = result[:, row * cols : (row + 1) * cols]
    lit = lit_ref[...]
    other = pltpu.roll(lit, half, 0)
    lit = jnp.where(low, other, lit) if north else jnp.where(low, lit, other)

    def body(step, carry):
        value = spread[pl.ds(step * 10 * rows, 10 * rows), :].reshape(10, rows, cols)
        value = jnp.where(lit > 0.5, value.astype(BF16).astype(F32), 0.0)
        held = half_tiles(state_ref[pl.ds(first + step * 20, 20)], low, north)
        tracer_ref[pl.ds(step * 5, 5)] = tall(held + PHYSICS_STEP * value)
        return carry

    lax.fori_loop(0, levels // 20, body, 0, unroll=3)


def network_kernel(
    inner_ref,
    here_ref,
    north_ref,
    south_ref,
    rest_ref,
    one_ref,
    two_ref,
    three_ref,
    four_ref,
    five_ref,
    lit_ref,
    state_ref,
    winds_ref,
    upwind_ref,
    features,
    hidden_ref,
    tracer_ref,
    strips,
    spread,
):
    _, levels, rows, cols = inner_ref.shape
    per = cols // STRIP
    packs = levels // per
    parts = [here_ref[pl.ds(field * packs, packs)] for field in range(3)]
    parts += [short(ref, 0, packs) for ref in (north_ref, south_ref)]
    for field, value in enumerate(substeps(*parts, open_rows(rows, cols))):
        strips[field] = value
    lane = iota((rows, cols), 1)

    def merge(step, carry):
        for slot in range(per):
            level = step * per + slot
            for field in range(3):
                strip = strips[field, step]
                west = pltpu.roll(strip, back(slot * STRIP + 4 * SUBSTEPS, cols), 1)
                east = pltpu.roll(strip, back(slot * STRIP + 2 * SUBSTEPS, cols), 1)
                value = inner_ref[field, level]
                value = jnp.where(lane < SUBSTEPS, west, value)
                value = jnp.where(lane >= cols - SUBSTEPS, east, value)
                winds_ref[pl.ds((field * levels + level) * rows, rows), :] = value
                if field == 0:
                    upwind_ref[level] = pltpu.roll(jnp.where(lane == cols - 1, west, value), 1, 1)
        return carry

    lax.fori_loop(0, packs, merge, 0, unroll=packs)
    count = 3 * levels
    features[...] = rest_ref[...]
    for row in range(rows):
        features[0:count, row * cols : (row + 1) * cols] = winds_ref[
            pl.ds(row, count, stride=rows), :
        ].astype(BF16)
    half_step(
        features,
        (one_ref, two_ref, three_ref, four_ref),
        five_ref,
        lit_ref,
        state_ref,
        3 * levels,
        False,
        hidden_ref,
        tracer_ref,
        spread,
    )


def network(inner_out, strips, rest, layers, five, lit, flat):
    _, levels, rows, cols = inner_out.shape
    count = five.shape[0]
    return pl.pallas_call(
        network_kernel,
        out_shape=(
            jax.ShapeDtypeStruct((3 * levels * rows, cols), F32),
            jax.ShapeDtypeStruct((levels, rows, cols), F32),
            jax.ShapeDtypeStruct(rest.shape, BF16),
            jax.ShapeDtypeStruct((rows * cols // 2, layers[3].shape[1]), BF16),
            jax.ShapeDtypeStruct((count // 4, 2 * rows, cols), BF16),
        ),
        in_specs=[vmem()] * 12,
        out_specs=(vmem(),) * 5,
        scratch_shapes=[
            pltpu.VMEM((3, levels * STRIP // (cols - cols % STRIP), rows, cols), F32),
            pltpu.VMEM((count * rows // 2, cols), F32),
        ],
        compiler_params=params(32),
        cost_estimate=cost(3 << 30, 8 << 20),
    )(inner_out, *strips, rest, *layers, five, lit, flat)


def second_kernel(
    first, features_ref, one_ref, two_ref, three_ref, four_ref, five_ref, lit_ref, state_ref,
    hidden_ref, tracer_ref, spread,
):
    layers = (one_ref, two_ref, three_ref, four_ref)
    half_step(
        features_ref, layers, five_ref, lit_ref, state_ref, first, True, hidden_ref, tracer_ref, spread
    )


def second(first, features, layers, five, lit, flat):
    rows, cols = lit.shape
    count = five.shape[0]
    return pl.pallas_call(
        functools.partial(second_kernel, first),
        out_shape=(
            jax.ShapeDtypeStruct((rows * cols // 2, layers[3].shape[1]), BF16),
            jax.ShapeDtypeStruct((count // 4, 2 * rows, cols), BF16),
        ),
        in_specs=[vmem()] * 8,
        out_specs=(vmem(),) * 2,
        scratch_shapes=[pltpu.VMEM((count * rows // 2, cols), F32)],
        compiler_params=params(24),
        cost_estimate=cost(2 << 30, 6 << 20),
    )(features, *layers, five, lit, flat)


def winds_kernel(
    south_ref, north_ref, five_ref, lit_ref, winds_ref, upwind_ref, out_ref, flux_ref,
    stay_ref, come_ref, stay_south_ref, come_south_ref, stay_north_ref, come_north_ref,
    spread, updated, sem
):
    rows, cols = lit_ref.shape
    levels = upwind_ref.shape[0]
    fluxes = flux_ref.shape[0]
    count = five_ref.shape[0]
    for side, hidden_ref in enumerate((south_ref, north_ref)):
        result = lax.dot_general(
            five_ref[...], hidden_ref[...], (((1,), (1,)), ((), ())), preferred_element_type=F32
        )
        for row in range(rows // 2):
            spread[pl.ds(side * (rows // 2) + row, count, stride=rows), :] = result[
                :, row * cols : (row + 1) * cols
            ]
    lit = lit_ref[...] > 0.5
    low = iota((rows, cols), 0) < rows // 2

    def body(step, carry):
        value = spread[pl.ds(step * 10 * rows, 10 * rows), :].reshape(10, rows, cols)
        value = jnp.where(lit, value.astype(BF16).astype(F32), 0.0)
        wind = winds_ref[pl.ds(step * 10 * rows, 10 * rows), :].reshape(10, rows, cols)
        updated[pl.ds(step * 10, 10)] = wind + PHYSICS_STEP * value
        return carry

    lax.fori_loop(0, 2 * levels // 10, body, 0)
    updated[2 * levels : 3 * levels] = winds_ref[2 * levels * rows :, :].reshape(
        levels, rows, cols
    )
    copy = pltpu.make_async_copy(
        updated, out_ref.at[pl.ds(0, 3 * levels)], sem
    )
    copy.start()
    value = spread[2 * levels * rows :, :].reshape(fluxes, rows, cols)
    flux_ref[...] = jnp.where(lit, value, 0.0).astype(BF16)

    def share(step, carry):
        here = winds_ref[pl.ds(step * 10 * rows, 10 * rows), :].reshape(10, rows, cols)
        stay = 0.5 - 0.45 * jnp.tanh(here)
        come = 0.5 + 0.45 * jnp.tanh(upwind_ref[pl.ds(step * 10, 10)])
        stay_ref[pl.ds(step * 10, 10)] = stay
        come_ref[pl.ds(step * 10, 10)] = come
        stay_south_ref[pl.ds(step * 5, 5)] = half_tiles(stay, low, False)
        come_south_ref[pl.ds(step * 5, 5)] = half_tiles(come, low, False)
        stay_north_ref[pl.ds(step * 5, 5)] = half_tiles(stay, low, True)
        come_north_ref[pl.ds(step * 5, 5)] = half_tiles(come, low, True)
        return carry

    lax.fori_loop(0, levels // 10, share, 0)
    copy.wait()


def winds_out(hidden_south, hidden_north, five, lit, winds, upwind, fields):
    levels, rows, cols = upwind.shape
    fluxes = five.shape[0] - 2 * levels
    share = jax.ShapeDtypeStruct((levels, rows, cols), F32)
    part = jax.ShapeDtypeStruct((levels // 2, rows, cols), F32)
    return pl.pallas_call(
        winds_kernel,
        out_shape=(
            jax.ShapeDtypeStruct((fields * levels, rows, cols), F32),
            jax.ShapeDtypeStruct((fluxes, rows, cols), BF16),
            share,
            share,
            part,
            part,
            part,
            part,
        ),
        in_specs=[vmem()] * 6,
        out_specs=(any_space(),) + (vmem(),) * 7,
        scratch_shapes=[
            pltpu.VMEM((five.shape[0] * rows, cols), F32),
            pltpu.VMEM((3 * levels, rows, cols), F32),
            pltpu.SemaphoreType.DMA,
        ],
        compiler_params=params(16),
        cost_estimate=cost(1 << 28, 4 << 20),
    )(hidden_south, hidden_north, five, lit, winds, upwind)


def spread_offsets(offset_ref, shape, base, span):
    rows, cols = shape
    place = iota((rows, cols), 0) % span
    offset = jnp.zeros((rows, cols), jnp.int32)
    for row in range(span):
        offset = jnp.where(place == row, offset_ref[base + row], offset)
    return offset // cols, offset % cols


def along(value, index):
    return jnp.take_along_axis(value, index, axis=1, mode="promise_in_bounds")


def relay_kernel(base, span, offset_ref, own_ref, near_ref, out_ref, column_ref):
    rows = own_ref.shape[1] // 2
    cols = own_ref.shape[2]
    pairs = own_ref.shape[0]
    blocks, cells = spread_offsets(offset_ref, (rows, cols), base, span)
    lane = iota((rows, cols), 1)
    take_near = (blocks >= 2) & (lane > cols - 1 - cells)
    edge = cols - 1 - cells

    def body(step, column):
        at = pl.ds(step * 10, 10)
        own = own_ref[at].astype(F32).reshape(20, rows, cols)
        near = near_ref[at].astype(F32).reshape(20, rows, cols)
        out_ref[at] = tall(jnp.where(take_near, near, own))
        source = jnp.where(blocks == 1, own, near)
        for level in range(20):
            column = jnp.where(lane == step * 20 + level, along(source[level], edge), column)
        return column

    steps = pairs // 10
    column = lax.fori_loop(0, steps, body, jnp.zeros((rows, cols), F32), unroll=3)
    out_ref[pairs] = jnp.concatenate([column, column], axis=0).astype(BF16)
    column_ref[...] = column


def relay(offset, own, near, base, span):
    pairs, height, cols = own.shape
    return pl.pallas_call(
        functools.partial(relay_kernel, base, span),
        out_shape=(
            jax.ShapeDtypeStruct((pairs + 1, height, cols), BF16),
            jax.ShapeDtypeStruct((height // 2, cols), F32),
        ),
        in_specs=[pl.BlockSpec(memory_space=pltpu.SMEM), vmem(), vmem()],
        out_specs=(vmem(), vmem()),
        compiler_params=params(8),
        cost_estimate=cost(1 << 20, 1 << 20),
    )(offset, own, near)


def blend(offset_ref, far_ref, column_ref, shape, base, span):
    rows, cols = shape
    blocks, cells = spread_offsets(offset_ref, shape, base, span)
    lane = iota((rows, cols), 1)
    from_right = lane <= cols - 1 - cells
    index = (lane - cells) & (cols - 1)
    is_zero, is_one = blocks == 0, blocks == 1
    sent = far_ref[far_ref.shape[0] - 1].astype(F32)[:rows]
    column = jnp.where(is_zero, column_ref[...], sent)

    def tiles(own, near, far, stay, come, first):
        right = jnp.where(is_zero, own, jnp.where(is_one, near, far))
        left = jnp.where(is_zero, near, far)
        merged = jnp.where(from_right, right, left)
        turned = pltpu.roll(column, lax.rem(cols - first, cols), 1)
        values = []
        for tile in range(own.shape[0]):
            here = along(merged[tile], index)
            edge = pltpu.roll(turned, back(tile, cols), 1)
            behind = jnp.where(lane == 0, edge, pltpu.roll(here, 1, 1))
            values.append(stay[tile] * here + come[tile] * behind)
        return values

    return tiles


def read_tiles(refs, step, group, shape):
    at = pl.ds(step * (group // 2), group // 2)
    return [ref[at].astype(F32).reshape((group,) + shape) for ref in refs]


def advect_ozone_kernel(
    first, offset_ref, own_ref, near_ref, far_ref, column_ref, stay_ref, come_ref, whole_ref, out_ref, result, sem
):
    levels, rows, cols = stay_ref.shape
    group = levels // 2
    tiles = blend(offset_ref, far_ref, column_ref, (rows, cols), 0, rows)
    copies = []
    for step in range(2):
        share = pl.ds(step * group, group)
        values = tiles(
            *read_tiles((own_ref, near_ref, far_ref), step, group, (rows, cols)),
            stay_ref[share],
            come_ref[share],
            step * group,
        )
        for tile, value in enumerate(values):
            result[step * group + tile] = value
        copy = pltpu.make_async_copy(
            result.at[share], out_ref.at[pl.ds(first * levels + step * group, group)], sem.at[step]
        )
        copy.start()
        copies.append(copy)
    for copy in copies:
        copy.wait()


def advect_ozone(first, offset, own, near, far, column, stay, come, whole):
    levels, rows, cols = stay.shape
    return pl.pallas_call(
        functools.partial(advect_ozone_kernel, first),
        out_shape=jax.ShapeDtypeStruct(whole.shape, F32),
        in_specs=[pl.BlockSpec(memory_space=pltpu.SMEM)] + [vmem()] * 6 + [any_space()],
        out_specs=any_space(),
        scratch_shapes=[pltpu.VMEM((levels, rows, cols), F32), pltpu.SemaphoreType.DMA((2,))],
        input_output_aliases={7: 0},
        compiler_params=params(8),
        cost_estimate=cost(1 << 22, 2 << 20),
    )(offset, own, near, far, column, stay, come, whole)


def advect_south_kernel(offset_ref, own_ref, near_ref, far_ref, column_ref, stay_ref, come_ref, out_ref):
    group, rows, cols = stay_ref.shape
    pairs = own_ref.shape[0]
    tiles = blend(offset_ref, far_ref, column_ref, (rows, cols), 0, rows // 2)

    def body(step, carry):
        values = tiles(
            *read_tiles((own_ref, near_ref, far_ref), step, group, (rows, cols)),
            stay_ref[...],
            come_ref[...],
            step * group,
        )
        for tile, value in enumerate(values):
            out_ref[step * group + tile] = value
        return carry

    lax.fori_loop(0, 2 * pairs // group, body, 0)


def advect_south(offset, own, near, far, column, stay, come):
    pairs, height, cols = own.shape
    return pl.pallas_call(
        advect_south_kernel,
        out_shape=jax.ShapeDtypeStruct((2 * pairs, height // 2, cols), F32),
        in_specs=[pl.BlockSpec(memory_space=pltpu.SMEM)] + [vmem()] * 6,
        out_specs=vmem(),
        compiler_params=params(8),
        cost_estimate=cost(1 << 22, 2 << 20),
    )(offset, own, near, far, column, stay, come)


def advect_north_kernel(
    first, offset_ref, own_ref, near_ref, far_ref, column_ref, stay_ref, come_ref, south_ref, whole_ref, out_ref,
    result, sem,
):
    group, rows, cols = stay_ref.shape
    pairs = own_ref.shape[0]
    tiles = blend(offset_ref, far_ref, column_ref, (rows, cols), rows // 2, rows // 2)
    low = iota((rows, cols), 0) < rows // 2
    count = 2 * pairs // group

    def copy_of(step):
        span = pl.ds(step * 2 * group, 2 * group)
        return pltpu.make_async_copy(
            result.at[span],
            out_ref.at[pl.ds((first + step) * 2 * group, 2 * group)],
            sem.at[step],
        )

    def body(step, carry):
        values = tiles(
            *read_tiles((own_ref, near_ref, far_ref), step, group, (rows, cols)),
            stay_ref[...],
            come_ref[...],
            step * group,
        )
        for tile, north in enumerate(values):
            at = step * group + tile
            south = south_ref[at]
            result[2 * at] = jnp.where(low, south, pltpu.roll(north, rows // 2, 0))
            result[2 * at + 1] = jnp.where(low, pltpu.roll(south, rows // 2, 0), north)
        copy_of(step).start()
        return carry

    lax.fori_loop(0, count, body, 0)
    for step in range(count):
        copy_of(step).wait()


def advect_north(first, offset, own, near, far, column, stay, come, south, whole):
    pairs, height, cols = own.shape
    count = 2 * pairs // stay.shape[0]
    return pl.pallas_call(
        functools.partial(advect_north_kernel, first),
        out_shape=jax.ShapeDtypeStruct(whole.shape, F32),
        in_specs=[pl.BlockSpec(memory_space=pltpu.SMEM)] + [vmem()] * 7 + [any_space()],
        out_specs=any_space(),
        scratch_shapes=[
            pltpu.VMEM((4 * pairs, height // 2, cols), F32),
            pltpu.SemaphoreType.DMA((count,)),
        ],
        input_output_aliases={8: 0},
        compiler_params=params(16),
        cost_estimate=cost(1 << 22, 4 << 20),
    )(offset, own, near, far, column, stay, come, south, whole)


def shifted(value, axis, steps):
    count = lax.axis_size(axis)
    return lax.ppermute(value, axis, [(i, (i + steps) % count) for i in range(count)])


def on_device(
    state,
    surface,
    layer_one,
    layer_two,
    layer_three,
    layer_four,
    layer_five,
    lit_columns,
    row_offset,
):
    return tile_step(
        state,
        surface,
        (layer_one, layer_two, layer_three, layer_four),
        layer_five,
        lit_columns,
        row_offset,
    )


def tile_step(state, surface, layers, layer_five, lit_columns, row_offset):
    fields, levels, rows, cols = state.shape
    slots = lit_columns.reshape(1, rows * cols)
    flat = state.reshape(fields * levels, rows, cols)

    start_winds = state[:3]
    to_south, to_north, to_west, to_east = messages(start_winds)
    rest, lit, ozone = rest_features(state, surface, slots)
    from_east = shifted(to_west, "lon", -1)
    from_west = shifted(to_east, "lon", 1)
    from_south = shifted(to_north, "lat", 1)
    from_north = shifted(to_south, "lat", -1)
    ozone_near = shifted(ozone, "lon", 1)
    strips, strips_south, strips_north = strips_of(to_west, to_east, from_east, from_west)
    strips_from_south = shifted(strips_north, "lat", 1)
    strips_from_north = shifted(strips_south, "lat", -1)

    five = layer_five.T
    five_tracers = five[2 * levels : 6 * levels]
    five_winds = jnp.concatenate([five[: 2 * levels], five[6 * levels :]], axis=0)

    inner_out = inner(start_winds, from_north, from_south)
    ozone_relay, ozone_column = relay(row_offset, ozone, ozone_near, 0, rows)
    ozone_far = shifted(ozone_relay, "lon", 2)
    winds, upwind, features, hidden_south, first = network(
        inner_out,
        (strips, strips_from_north, strips_from_south),
        rest,
        layers,
        five_tracers,
        lit,
        flat,
    )
    first_near = shifted(first, "lon", 1)
    hidden_north, other = second(3 * levels, features, layers, five_tracers, lit, flat)
    other_near = shifted(other, "lon", 1)
    first_relay, first_column = relay(row_offset, first, first_near, 0, rows // 2)
    first_far = shifted(first_relay, "lon", 2)
    other_relay, other_column = relay(row_offset, other, other_near, rows // 2, rows // 2)
    other_far = shifted(other_relay, "lon", 2)
    whole, flux, stay, come, stay_south, come_south, stay_north, come_north = winds_out(
        hidden_south, hidden_north, five_winds, lit, winds, upwind, fields
    )
    whole = advect_ozone(
        fields - 1, row_offset, ozone, ozone_near, ozone_far, ozone_column, stay, come, whole
    )
    south = advect_south(row_offset, first, first_near, first_far, first_column, stay_south, come_south)
    whole = advect_north(
        3, row_offset, other, other_near, other_far, other_column, stay_north, come_north, south, whole
    )
    return whole.reshape(fields, levels, rows, cols), flux


def solution(mesh):
    in_specs = (
        P(None, None, "lat", "lon"),
        P(None, "lat", "lon"),
        P(),
        P(),
        P(),
        P(),
        P(),
        P("lat", "lon", None),
        P("lat"),
    )
    out_specs = (P(None, None, "lat", "lon"), P(None, "lat", "lon"))
    return jax.shard_map(
        on_device, mesh=mesh, in_specs=in_specs, out_specs=out_specs, check_vma=False
    )
```
